256 devices in a mesh: dp: 8 (over y_hi, x), ctx: 32 (over y_lo, z, core).
Axes of the slice: x: 4, y: 4 (y_hi: 2, y_lo: 2; y = y_hi * 2 + y_lo), z: 8, core: 2. Of those that a mesh axis runs over, the one named last changes fastest.
Arguments:
- mixed: bfloat16 [8192, 4096], P('ctx', 'dp'), may hold values from -6 to 6
- log_decay: float32 [8192, 16], P('ctx', 'dp'), may hold values from -1 to 0
- beta_logit: float32 [8192, 16], P('ctx', 'dp'), may hold values from -4 to 4
- conv_weight: float32 [4, 4096], P(None, 'dp'), may hold values from -3 to 3
- norm_gain: float32 [128], replicated, may hold values from 0.1 to 1.9
- out_weight: bfloat16 [2048, 1024], P('dp'), may hold values from -0.125 to 0.125
- out_grad: bfloat16 [8192, 1024], P(('ctx', 'dp')), may hold values from -12 to 12
Outputs:
- output: bfloat16 [8192, 1024], P(('ctx', 'dp'))
- grad_mixed: bfloat16 [8192, 4096], P('ctx', 'dp')
- grad_log_decay: float32 [8192, 16], P('ctx', 'dp')
- grad_beta_logit: float32 [8192, 16], P('ctx', 'dp')
- grad_conv_weight: float32 [4, 4096], P(None, 'dp')
- grad_norm_gain: float32 [128], replicated
- grad_out_weight: float32 [2048, 1024], P(('dp', 'ctx'))
The draws below stay inside these ranges and needn't reach their ends.
All inputs are finite; a program needn't handle non-finite values.
Results may differ from the reference program's by a relative error of at most 0.03.
Values may be sent and summed in bfloat16 or wider, within the bound.
No kernel may reach another device: no remote copies, remote signals or barrier semaphores. Data moves between devices by JAX's collectives and lax.ppermute only.
A program may use at most 128 MiB of HBM per device.

```python
import math
import jax
import jax.numpy as jnp
from jax import lax

VHEADS = 16
KHEADS = 8
HEADDIM = 128
DWIN = 1024
CONV = 4
BLOCK = 64
SEQUENCE_LENGTH = 8192
VDIM = 2048
QKV = 4096


def draw_log_decay(key, part):
    head_random_key, retain_random_key, quick_decay_key, noise_random_key, spike_random_key, loss_random_key = jax.random.split(key, 6)
    fast_share = 0.5
    fast_heads = jax.random.uniform(head_random_key, (1, VHEADS), jnp.float32) < fast_share
    kept_share = jax.random.uniform(retain_random_key, (1, VHEADS), jnp.float32, minval=0.4, maxval=0.8)
    slow_rate = -jnp.log(kept_share) / SEQUENCE_LENGTH
    fast_rate = jax.random.uniform(quick_decay_key, (1, VHEADS), jnp.float32, minval=1.0 / 50.0, maxval=1.0 / 30.0)
    decay_rate = jnp.where(fast_heads, fast_rate, slow_rate)
    jitter = jnp.exp(jax.random.uniform(noise_random_key, (SEQUENCE_LENGTH, VHEADS), jnp.float32, minval=math.log(0.5), maxval=math.log(2.0)))
    spike_token_rows = jax.random.randint(spike_random_key, (1, 2), 0, SEQUENCE_LENGTH)
    token_position = lax.broadcasted_iota(jnp.int32, (SEQUENCE_LENGTH, 2), 0)
    spike_row_mask = jnp.any(token_position == spike_token_rows, axis=-1, keepdims=True)
    loss_component = jax.random.uniform(loss_random_key, (SEQUENCE_LENGTH, VHEADS), jnp.float32, minval=math.log(0.6), maxval=math.log(0.8))
    stable_rows = -decay_rate * jitter
    return jnp.where(spike_row_mask, stable_rows + loss_component, stable_rows)


def draw_out_grad(key, part):
    noise_part = jnp.clip(jax.random.normal(key, (SEQUENCE_LENGTH, DWIN), jnp.float32), -5.0, 5.0)
    token_position = lax.broadcasted_iota(jnp.float32, (SEQUENCE_LENGTH, 1), 0) / SEQUENCE_LENGTH
    row_scale = 0.5 + token_position
    return (noise_part * row_scale).astype(jnp.bfloat16)


def block_levels(own_key, dims, pieces, least, high):
    level, own = 1.0, jax.random.fold_in(own_key, 6)
    for axis_at, shards_of in pieces:
        heights = jnp.exp(jax.random.uniform(jax.random.fold_in(own, axis_at), (shards_of,), jnp.float32, least / len(pieces), high / len(pieces)))
        level = level * jnp.repeat(heights, dims[axis_at] // shards_of).reshape([-1 if axis == axis_at else 1 for axis in range(len(dims))])
    return level


def centred(rng, dims, deviation, most, shards=(), dtype=jnp.bfloat16):
    factor_of = block_levels(rng, dims, shards, -0.22, 0.18) if shards else 1.0
    values = jax.random.normal(rng, dims, jnp.float32) * deviation * factor_of
    return jnp.minimum(jnp.maximum(values, -most), most).astype(dtype)


def setup_inputs(seed: int = 0) -> dict:
    seeds = jax.random.split(jax.random.key(seed), 8)
    return {
        "mixed": centred(seeds[0], (SEQUENCE_LENGTH, QKV), 1.0, 6.0, ((0, 32), (1, 8))),
        "log_decay": draw_log_decay(jax.random.fold_in(seeds[7], 71), 0),
        "beta_logit": centred(seeds[2], (SEQUENCE_LENGTH, VHEADS), 1.0, 4.0, ((0, 32), (1, 8)), jnp.float32),
        "conv_weight": centred(seeds[3], (CONV, QKV), CONV ** -0.5, 3.0, ((1, 8),), jnp.float32),
        "norm_gain": jnp.clip(1.0 + 0.18 * jax.random.normal(seeds[4], (HEADDIM,), jnp.float32), 0.1, 1.9),
        "out_weight": centred(seeds[5], (VDIM, DWIN), VDIM ** -0.5, 0.125, ((0, 8),)),
        "out_grad": draw_out_grad(jax.random.fold_in(seeds[7], 71), 0),
    }


EPS = 1e-06
HIGHEST = lax.Precision.HIGHEST

def product(pattern, left_array, right_array):
    return jnp.einsum(pattern, left_array, right_array, precision=HIGHEST)

def conv_silu(padded_rows, conv_weight):
    conv_taps = conv_weight.shape[0]
    row_count = padded_rows.shape[0] - (conv_taps - 1)
    summed = jnp.zeros((row_count, padded_rows.shape[1]), jnp.float32)
    for offset in range(conv_taps):
        summed = summed + conv_weight[offset] * padded_rows[offset:offset + row_count]
    return jax.nn.silu(summed)

def unit_rows(vectors):
    return vectors * lax.rsqrt(lax.optimization_barrier(jnp.sum(vectors * vectors, axis=-1, keepdims=True)) + EPS)

def prepare(active, decays, strengths):
    row_count = active.shape[0]
    value_heads = decays.shape[1]
    group_size = VHEADS // KHEADS
    key_heads = value_heads // group_size
    grouped = active.reshape(row_count, key_heads, (2 + group_size) * HEADDIM)
    queries = unit_rows(grouped[:, :, :HEADDIM]) * (1.0 / math.sqrt(HEADDIM))
    key_rows = unit_rows(grouped[:, :, HEADDIM:2 * HEADDIM])
    values = grouped[:, :, 2 * HEADDIM:].reshape(row_count, value_heads, HEADDIM)
    queries = jnp.repeat(queries, group_size, axis=1)
    key_rows = jnp.repeat(key_rows, group_size, axis=1)
    blocks = row_count // BLOCK

    def arrange(tensor):
        return jnp.transpose(tensor.reshape(blocks, BLOCK, value_heads, -1), (0, 2, 1, 3))
    return (arrange(queries), arrange(key_rows), arrange(values), arrange(decays[:, :, None])[..., 0], arrange(jax.nn.sigmoid(strengths)[:, :, None])[..., 0])

def block_terms(block_in):
    queries, key_rows, values, decays, strengths = (block_in[0], block_in[1], block_in[2], block_in[3], block_in[4])
    length = decays.shape[-1]
    cumulative = jnp.cumsum(decays, axis=-1)
    row_index = lax.broadcasted_iota(jnp.int32, (length, length), 0)
    col_index = lax.broadcasted_iota(jnp.int32, (length, length), 1)
    causal = row_index >= col_index
    strict = row_index > col_index
    spread = cumulative[:, :, None] - cumulative[:, None, :]
    damping = jnp.where(causal, jnp.exp(jnp.where(causal, spread, 0.0)), 0.0)
    key_inner = product('hck,hsk->hcs', key_rows, key_rows)
    lower_mat = jnp.where(strict, strengths[:, :, None] * damping * key_inner, 0.0)
    growth = jnp.exp(cumulative)
    tail_keys = jnp.exp(cumulative[:, -1:] - cumulative)[..., None] * key_rows
    stacked = jnp.concatenate([(strengths * growth)[..., None] * key_rows, strengths[..., None] * values], axis=-1)
    solved = lax.linalg.triangular_solve(lower_mat, stacked, left_side=True, lower=True, unit_diagonal=True)
    head_size = key_rows.shape[-1]
    write_keys = solved[..., :head_size]
    new_values = solved[..., head_size:]
    scores = damping * product('hck,hsk->hcs', queries, key_rows)
    return (write_keys, new_values, scores, growth, tail_keys, queries, growth[:, -1])

def rows_layout(stacked):
    return jnp.transpose(stacked, (0, 2, 1, 3)).reshape(stacked.shape[0] * stacked.shape[2], stacked.shape[1], stacked.shape[3])

def run_blocks(carry_state, arranged):

    def advance(running, block_in):
        write_keys, new_values, scores, growth, tail_keys, queries, growth_end = block_terms(block_in)
        deltas = new_values - product('hck,hek->hce', write_keys, running)
        output = growth[..., None] * product('hck,hek->hce', queries, running) + product('hcs,hse->hce', scores, deltas)
        next_state = growth_end[:, None, None] * running + product('hse,hsk->hek', deltas, tail_keys)
        return (next_state, output)
    final_state, outputs = lax.scan(advance, carry_state, arranged)
    return (rows_layout(outputs), final_state)

def normalize(mixer_out, gain_vector):
    scaled = mixer_out * lax.rsqrt(lax.optimization_barrier(jnp.mean(mixer_out * mixer_out, axis=-1, keepdims=True)) + EPS) * gain_vector
    return scaled.reshape(mixer_out.shape[0], -1)

def full_core(active, decays, strengths, gain_vector):
    start_state = jnp.zeros((decays.shape[1], HEADDIM, HEADDIM), jnp.float32)
    mixer_out, final_state = run_blocks(start_state, prepare(active, decays, strengths))
    return normalize(mixer_out, gain_vector)

def reference(mixed, log_decay, beta_logit, conv_weight, norm_gain, out_weight, out_grad):
    padded = jnp.concatenate([jnp.zeros((CONV - 1, mixed.shape[1]), jnp.float32), mixed.astype(jnp.float32)], axis=0)
    active_wide, conv_pull = jax.vjp(conv_silu, padded, conv_weight)
    active = lax.optimization_barrier(active_wide.astype(jnp.bfloat16)).astype(jnp.float32)
    normed_wide, core_pull = jax.vjp(full_core, active, log_decay, beta_logit, norm_gain)
    normed = normed_wide.astype(jnp.bfloat16)
    result = jnp.dot(normed.astype(jnp.float32), out_weight.astype(jnp.float32), preferred_element_type=jnp.float32).astype(jnp.bfloat16)
    back_rows = jnp.dot(out_grad.astype(jnp.float32), out_weight.T.astype(jnp.float32), preferred_element_type=jnp.float32)
    weight_grad = jnp.dot(normed.T.astype(jnp.float32), out_grad.astype(jnp.float32), preferred_element_type=jnp.float32)
    grad_active, grad_decay, grad_beta, grad_gain = core_pull(back_rows)
    grad_padded, grad_conv = conv_pull(grad_active)
    return (result, grad_padded[CONV - 1:].astype(jnp.bfloat16), grad_decay, grad_beta, grad_conv, grad_gain, weight_grad)
```

```python
import functools
import math

import jax
import jax.numpy as jnp
from jax import lax
from jax.experimental import pallas as pl
from jax.experimental.pallas import tpu as pltpu
from jax.sharding import Mesh
from jax.sharding import PartitionSpec as P

D = 128
ROWS = 256
NB = 4
EPS = 1e-06
SCALE = 1.0 / math.sqrt(D)
HIGHEST = lax.Precision.HIGHEST
F32 = jnp.float32
BF16 = jnp.bfloat16
PACK = 272

FORMS = {
    "nn": (((1,), (0,)), ((), ())),
    "nt": (((1,), (1,)), ((), ())),
    "tn": (((0,), (0,)), ((), ())),
}


def halves(x):
    high = x.astype(BF16)
    return high, (x - high.astype(F32)).astype(BF16)


def mm(a, b, form="nn", passes=1):
    dims = FORMS[form]
    dot = functools.partial(lax.dot_general, dimension_numbers=dims, preferred_element_type=F32)
    if passes == 6:
        return dot(a, b, precision=HIGHEST)
    if passes == 1:
        return dot(a.astype(BF16), b.astype(BF16))
    ah, al = halves(a)
    bh, bl = halves(b)
    return dot(ah, bh) + (dot(ah, bl) + dot(al, bh))


P_KK = 3
P_INV = 3
P_TY = 3
P_MAP = 1
P_OUT = 1
P_BACK = 1


def grid_index():
    return (
        lax.broadcasted_iota(jnp.int32, (D, D), 0),
        lax.broadcasted_iota(jnp.int32, (D, D), 1),
    )


def row_sum(x):
    return jnp.sum(x, axis=-1, keepdims=True)


def triangle_inverses(lowers):
    i, j = grid_index()
    eye = (i == j).astype(F32)
    small = [jnp.where((i >> 3) == (j >> 3), low, 0.0) for low in lowers]
    squares = [mm(s, s, passes=P_INV) for s in small]
    cubes = [mm(s, q, passes=P_INV) for s, q in zip(small, squares)]
    fourths = [mm(q, q, passes=P_INV) for q in squares]
    starts = [eye - s + q - c for s, q, c in zip(small, squares, cubes)]
    inverses = [t + mm(t, f, passes=P_INV) for t, f in zip(starts, fourths)]
    for level in (3, 4, 5, 6):
        joint = ((i >> (level + 1)) == (j >> (level + 1))) & ((i >> level) > (j >> level))
        inner = [
            mm(jnp.where(joint, low, 0.0), t, passes=P_INV) for low, t in zip(lowers, inverses)
        ]
        inverses = [t - mm(t, c, passes=P_INV) for t, c in zip(inverses, inner)]
    return inverses


def silu(u):
    return u / (1.0 + jnp.exp(-u))


def unit(raw):
    inverse = lax.rsqrt(row_sum(raw * raw) + EPS)
    return raw * inverse, inverse


def block(b):
    return slice(b * D, (b + 1) * D)


def value_lanes(core):
    return pl.ds(pl.multiple_of(2 * D + core * D, D), D)


def lane_groups(core):
    return (slice(0, D), slice(D, 2 * D), value_lanes(core))


def damping(cum_col, cum_row):
    i, j = grid_index()
    causal = i >= j
    return jnp.where(causal, jnp.exp(jnp.where(causal, cum_col - cum_row, 0.0)), 0.0)


def gate_columns(gates):
    return jnp.transpose(gates)


def maps_kernel(
    ids, mixed, other, tail_a, tail_b, gate_own, gate_other, conv_w,
    padded, pre, q_out, k_out, inverse_out, x_out, scores_out, maps_out, gates_out, packed,
):
    core = ids[1]
    for group, lanes in enumerate(lane_groups(core)):
        here = slice(group * D, (group + 1) * D)
        padded[0:8, here] = jnp.zeros((8, D), F32)
        padded[5:8, here] = tail_a[:, lanes].astype(F32) + tail_b[:, lanes].astype(F32)
        padded[pl.ds(8 + core * ROWS, ROWS), here] = mixed[:, lanes].astype(F32)
        padded[pl.ds(8 + (1 - core) * ROWS, ROWS), here] = other[:, lanes].astype(F32)

    gates_out[...] = jnp.zeros_like(gates_out)
    for source, own in ((gate_own, True), (gate_other, False)):
        picked = jnp.where(core == 0, source[...], pltpu.roll(source[...], 7, 0))
        at = (core if own else 1 - core) * 2
        for half in range(2):
            gates_out[pl.ds(at + half, 1), :] = picked[0:1, block(half)]
            gates_out[pl.ds(4 + at + half, 1), :] = picked[2:3, block(half)]
    i, j = grid_index()
    raw = gates_out[...]
    upto = (i <= j).astype(F32)
    cumulative = mm(raw, upto, passes=6)
    is_decay = lax.broadcasted_iota(jnp.int32, (8, D), 0) < 4
    gates = jnp.where(is_decay, cumulative, 1.0 / (1.0 + jnp.exp(-raw)))
    gates_out[...] = gates
    columns = gate_columns(gates)

    qs, ks, vs = [], [], []
    for b in range(NB):
        pieces = []
        for group, lanes in enumerate(lane_groups(core)):
            here = slice(group * D, (group + 1) * D)
            total = conv_w[0:1, lanes] * padded[5 + b * D : 5 + (b + 1) * D, here]
            for tap in range(1, 4):
                start = 5 + tap + b * D
                total = total + conv_w[tap : tap + 1, lanes] * padded[start : start + D, here]
            pre[block(b), here] = total
            pieces.append(silu(total).astype(BF16).astype(F32))
        q = unit(pieces[0])[0] * SCALE
        k = unit(pieces[1])[0]
        q_out[block(b), :] = q
        k_out[block(b), :] = k
        qs.append(q)
        ks.append(k)
        vs.append(pieces[2])

    strict = i > j
    lowers = []
    for b in range(NB):
        damp = damping(columns[:, b : b + 1], gates[b : b + 1, :])
        both = mm(jnp.concatenate([ks[b], qs[b]], axis=0), ks[b], "nt", P_KK)
        lowers.append(jnp.where(strict, columns[:, 4 + b : 5 + b] * damp * both[0:D], 0.0))
        scores_out[block(b), :] = damp * both[D:]
    inverses = triangle_inverses(lowers)
    maps, decays = [], []
    for b in range(NB):
        inverse_out[block(b), :] = inverses[b]
        cum, beta = columns[:, b : b + 1], columns[:, 4 + b : 5 + b]
        stacked = jnp.concatenate([(beta * jnp.exp(cum)) * ks[b], beta * vs[b]], axis=1)
        x = mm(inverses[b], stacked, passes=P_TY)
        x_out[block(b), :] = x
        end = gates[b : b + 1, D - 1 : D]
        tail_keys = jnp.exp(end - cum) * ks[b]
        both = mm(x, tail_keys, "tn", P_MAP)
        maps_out[2 * b * D : 2 * (b + 1) * D, :] = both
        maps.append(both)
        decays.append(jnp.exp(end))

    def compose(first, first_decay, then, then_decay):
        moved = mm(first, then[0:D], passes=P_MAP)
        through = then_decay * first[0:D] + first_decay * then[0:D] - moved[0:D]
        added = then_decay * first[D:] - moved[D:] + then[D:]
        return jnp.concatenate([through, added], axis=0), first_decay * then_decay

    early, early_decay = compose(maps[0], decays[0], maps[1], decays[1])
    late, late_decay = compose(maps[2], decays[2], maps[3], decays[3])
    whole, decay = compose(early, early_decay, late, late_decay)
    whole = whole.astype(BF16)
    row = lax.broadcasted_iota(jnp.int32, (16, D), 0)
    decay = jnp.broadcast_to(decay, (16, D))
    high = decay.astype(BF16).astype(F32)
    low = (decay - high).astype(BF16).astype(F32)
    lowest = decay - high - low
    parts = jnp.where(row == 0, high, jnp.where(row == 1, low, jnp.where(row == 2, lowest, 0.0)))
    parts = parts.astype(BF16)
    for copy in range(packed.shape[0]):
        packed[copy, 0 : 2 * D, :] = whole
        packed[copy, 2 * D : PACK, :] = parts


def readout_kernel(scores, x, q, gates, read_out, base_out):
    columns = gate_columns(gates[...])
    for b in range(NB):
        px = mm(scores[block(b), :], x[block(b), :], passes=P_TY)
        grown = jnp.exp(columns[:, b : b + 1]) * q[block(b), :]
        read_out[2 * b * D : (2 * b + 1) * D, :] = grown - px[:, 0:D]
        read_out[(2 * b + 1) * D : 2 * (b + 1) * D, :] = -x[block(b), 0:D]
        base_out[2 * b * D : (2 * b + 1) * D, :] = px[:, D:]
        base_out[(2 * b + 1) * D : 2 * (b + 1) * D, :] = x[block(b), D:]


def back_kernel(ids, full_grad, weight, back_out):
    rows = weight[pl.ds(pl.multiple_of(ids[1] * D, D), D), :]
    back_out[...] = mm(full_grad[...], rows, "nt")


def slab_decay(piece):
    return jnp.sum(piece[2 * D : PACK].astype(F32), axis=0, keepdims=True)


def outputs_kernel(
    ids, gathered, maps, read, base, gates, back, gain,
    states_out, deltas_out, grads_out, reach_out, packed_grad, normed_out, sent, gain_out,
):
    chip, core = ids[0], ids[1]

    def fold(position, state):
        piece = gathered[position]
        return slab_decay(piece) * state + (
            piece[D : 2 * D].astype(F32) - mm(state, piece[0:D], passes=P_MAP)
        )

    state = lax.fori_loop(0, chip, fold, jnp.zeros((D, D), F32))
    states, decays = [], []
    for b in range(NB):
        states.append(state)
        states_out[block(b), :] = state
        decay = jnp.exp(gates[b : b + 1, D - 1 : D])
        decays.append(decay)
        if b + 1 < NB:
            here = maps[2 * b * D : 2 * (b + 1) * D, :]
            state = decay * state - mm(state, here[0:D], passes=P_MAP) + here[D:]
    total_gain = jnp.zeros((1, D), F32)
    reaches = []
    for b in range(NB):
        both = slice(2 * b * D, 2 * (b + 1) * D)
        rows = base[both, :] + mm(read[both, :], states[b], "nt", P_OUT)
        out = rows[0:D]
        deltas_out[block(b), :] = rows[D:]
        inverse = lax.rsqrt(row_sum(out * out) * (1.0 / D) + EPS)
        unit_out = out * inverse
        normed = (unit_out * gain[...]).astype(BF16)
        normed_out[block(b), :] = normed

        @pl.when((b // 2) != core)
        def _():
            sent[block(b % 2), :] = normed

        cotangent = back[block(b), :]
        total_gain = total_gain + jnp.sum(cotangent * unit_out, axis=0, keepdims=True)
        scaled = cotangent * gain[...]
        grad = inverse * (scaled - unit_out * (row_sum(scaled * unit_out) * (1.0 / D)))
        grads_out[block(b), :] = grad
        reach = mm(grad, read[2 * b * D : (2 * b + 1) * D, :], "tn", P_OUT)
        reach_out[block(b), :] = reach
        reaches.append(reach)
    gain_out[...] = jnp.broadcast_to(total_gain, (8, D))
    state_grad = reaches[NB - 1]
    for b in range(NB - 2, -1, -1):
        through = maps[2 * b * D : (2 * b + 1) * D, :]
        state_grad = decays[b] * state_grad - mm(state_grad, through, "nt", P_MAP) + reaches[b]
    state_grad = state_grad.astype(BF16)
    for copy in range(packed_grad.shape[0]):
        packed_grad[copy] = state_grad


def local_grads_kernel(
    scores, deltas, grads, states, q, k, gates,
    dq_out, dk_out, pull_out, rows_out, sums_out,
):
    columns = gate_columns(gates[...])
    i, j = grid_index()
    sums_out[...] = jnp.zeros_like(sums_out)
    for b in range(NB):
        at = block(b)
        grad, score = grads[at, :], scores[at, :]
        damp = damping(columns[:, b : b + 1], gates[b : b + 1, :])
        d_score = jnp.where(i >= j, mm(grad, deltas[at, :], "nt", P_BACK), 0.0)
        d_inner = d_score * damp
        sums_out[b : b + 1, :] = jnp.sum(d_score * score, axis=0, keepdims=True)
        reading = mm(grad, states[at, :], passes=P_BACK)
        growth = jnp.exp(columns[:, b : b + 1])
        dq_out[at, :] = growth * reading + mm(d_inner, k[at, :], passes=P_BACK)
        dk_out[at, :] = mm(d_inner, q[at, :], "tn", P_BACK)
        pull_out[at, :] = mm(score, grad, "tn", P_BACK)
        row = row_sum(d_score * score) + row_sum(growth * q[at, :] * reading)
        rows_out[at, :] = jnp.broadcast_to(row, (D, D))


def grads_kernel(
    ids, gathered, gathered_grad, maps, reach, states, deltas, inverse, x, q, k, gates, pre, padded,
    dq, dk, pull, rows_in, sums, conv_w,
    keep_out, send_out, spill_out, gate_keep, gate_send, conv_out,
    d_pre,
):
    chip, core = ids[0], ids[1]
    count = gathered.shape[0]

    def fold(step, total):
        position = count - 1 - step
        piece = gathered[position]
        return slab_decay(piece) * total + (
            gathered_grad[position].astype(F32) - mm(total, piece[0:D], "nt", P_MAP)
        )

    exit_grad = lax.fori_loop(0, count - 1 - chip, fold, jnp.zeros((D, D), F32))
    columns = gate_columns(gates[...])
    i, j = grid_index()
    strict = i > j
    exits = [None] * NB
    decays = [jnp.exp(gates[b : b + 1, D - 1 : D]) for b in range(NB)]
    for b in range(NB - 1, -1, -1):
        exits[b] = exit_grad
        if b:
            through = maps[2 * b * D : (2 * b + 1) * D, :]
            exit_grad = (
                decays[b] * exit_grad - mm(exit_grad, through, "nt", P_MAP) + reach[block(b), :]
            )
    d_pre[NB * D : NB * D + 8, :] = jnp.zeros((8, 3 * D), F32)
    lane = lax.broadcasted_iota(jnp.int32, (D, D), 1)
    row_terms = jnp.zeros((D, D), F32)
    beta_terms = jnp.zeros((D, D), F32)
    col_rows, end_rows = [], []
    for b in range(NB):
        at = block(b)
        key, query = k[at, :], q[at, :]
        cum, beta = columns[:, b : b + 1], columns[:, 4 + b : 5 + b]
        growth = jnp.exp(cum)
        remain = jnp.exp(gates[b : b + 1, D - 1 : D] - cum)
        damp = damping(cum, gates[b : b + 1, :])
        tail_keys = remain * key
        d_delta = pull[at, :] + mm(tail_keys, exits[b], "nt", P_BACK)
        d_x = jnp.concatenate([-mm(d_delta, states[at, :], passes=P_BACK), d_delta], axis=1)
        d_y = mm(inverse[at, :], d_x, "tn", P_BACK)
        both = x[at, :]
        d_lower = jnp.where(strict, -mm(d_y, both, "nt", P_BACK), 0.0)
        d_inner = d_lower * (beta * damp)
        inner = mm(key, key, "nt", P_KK)
        elementwise = d_inner * inner
        d_tail = mm(deltas[at, :], exits[b], passes=P_BACK)
        symmetric = d_inner + jnp.transpose(d_inner)
        d_key = (
            dk[at, :]
            + mm(symmetric, key, passes=P_BACK)
            + (beta * growth) * d_y[:, 0:D]
            + remain * d_tail
        )
        d_query = dq[at, :]
        tail_dot = row_sum(d_tail * tail_keys)
        written = row_sum((beta * growth) * key * d_y[:, 0:D])
        row = rows_in[at, :] + (row_sum(elementwise) + written - tail_dot)
        row_terms = jnp.where(lane == b, row, row_terms)
        beta_terms = jnp.where(lane == b, (1.0 - beta) * row_sum(d_y * both), beta_terms)
        col_rows.append(sums[b : b + 1, :] + jnp.sum(elementwise, axis=0, keepdims=True))
        end = jnp.sum(tail_dot, axis=0, keepdims=True) + decays[b] * jnp.sum(
            row_sum(exits[b] * states[at, :]), axis=0, keepdims=True
        )
        end_rows.append(jnp.broadcast_to(end, (1, D)))

        u_q, u_k, u_v = pre[at, 0:D], pre[at, D : 2 * D], pre[at, 2 * D :]
        sigmoids = [1.0 / (1.0 + jnp.exp(-u)) for u in (u_q, u_k, u_v)]
        raw_q = (u_q * sigmoids[0]).astype(BF16).astype(F32)
        raw_k = (u_k * sigmoids[1]).astype(BF16).astype(F32)
        unit_q, inverse_q = unit(raw_q)
        inverse_k = unit(raw_k)[1]
        d_unit = d_query * SCALE
        d_raw_q = inverse_q * (d_unit - unit_q * row_sum(unit_q * d_unit))
        d_raw_k = inverse_k * (d_key - key * row_sum(key * d_key))
        d_raw_v = beta * d_y[:, D:]
        for group, (d_raw, u, s) in enumerate(
            zip((d_raw_q, d_raw_k, d_raw_v), (u_q, u_k, u_v), sigmoids)
        ):
            d_pre[at, group * D : (group + 1) * D] = d_raw * (s * (1.0 + u * (1.0 - s)))

    rows = jnp.transpose(row_terms)[0:8, :] - jnp.concatenate(
        col_rows + [jnp.zeros((4, D), F32)], axis=0
    )
    d_decay = mm(rows, (i >= j).astype(F32), passes=6) + jnp.concatenate(
        end_rows + [jnp.zeros((4, D), F32)], axis=0
    )
    d_logit = jnp.transpose(beta_terms)[0:8, :]
    for target, own in ((gate_keep, True), (gate_send, False)):
        target[...] = jnp.zeros_like(target)
        for head in range(2):

            @pl.when(core == head)
            def _():
                first = 2 * (head if own else 1 - head)
                for half in range(2):
                    b = first + half
                    target[head : head + 1, block(half)] = d_decay[b : b + 1, :]
                    target[2 + head : 3 + head, block(half)] = d_logit[b : b + 1, :]

    keep_out[...] = jnp.zeros_like(keep_out)
    send_out[...] = jnp.zeros_like(send_out)
    spill_out[...] = jnp.zeros_like(spill_out)
    conv_out[...] = jnp.zeros_like(conv_out)
    for group, lanes in enumerate(lane_groups(core)):
        here = slice(group * D, (group + 1) * D)
        taps = [conv_w[tap : tap + 1, lanes] for tap in range(4)]
        sums_of = [jnp.zeros((1, D), F32) for _ in range(4)]
        for b in range(NB):
            total = taps[3] * d_pre[b * D : (b + 1) * D, here]
            for tap in range(3):
                start = b * D + 3 - tap
                total = total + taps[tap] * d_pre[start : start + D, here]
            mine = (b // 2) == core
            at = slice((b % 2) * D, (b % 2 + 1) * D)

            @pl.when(mine)
            def _():
                keep_out[at, lanes] = total

            @pl.when(jnp.logical_not(mine))
            def _():
                send_out[at, lanes] = total.astype(BF16)

            for tap in range(4):
                start = 5 + tap + b * D
                sums_of[tap] = sums_of[tap] + jnp.sum(
                    d_pre[b * D : (b + 1) * D, here] * padded[start : start + D, here],
                    axis=0,
                    keepdims=True,
                )
        for tap in range(4):
            conv_out[tap : tap + 1, lanes] = sums_of[tap]
        for back in range(1, 4):
            total = jnp.zeros((1, D), F32)
            for tap in range(0, 4 - back):
                at = 3 - back - tap
                total = total + taps[tap] * d_pre[at : at + 1, here]
            spill_out[3 - back : 4 - back, lanes] = total


def project_kernel(ids, normed, received, weight, gain_part, out):
    core = ids[1]
    kept = normed[pl.ds(pl.multiple_of(core * ROWS, ROWS), ROWS), :]
    mine = weight[pl.ds(pl.multiple_of(core * D, D), D), :]
    others = weight[pl.ds(pl.multiple_of((1 - core) * D, D), D), :]
    share = (mm(kept, mine) + mm(received[...], others)).astype(BF16)
    count, height = out.shape[0], out.shape[1] - 16
    row = lax.broadcasted_iota(jnp.int32, (16, D), 0)
    gain = jnp.broadcast_to(gain_part[0:1, :], (16, D))
    high = gain.astype(BF16).astype(F32)
    extra = jnp.where(row == 0, high, jnp.where(row == 1, gain - high, 0.0)).astype(BF16)
    for owner in range(count):
        out[owner, 0:height, :] = share[owner * height : (owner + 1) * height]
        out[owner, height:, :] = jnp.zeros((16, out.shape[2]), BF16)
        out[owner, height:, 0:D] = extra


def call(kernel, shapes, args, name, flops, moved, scratch=(), smem=True):
    specs = [pl.BlockSpec(memory_space=pltpu.VMEM) for _ in args]
    if smem:
        specs[0] = pl.BlockSpec(memory_space=pltpu.SMEM)
    return pl.pallas_call(
        kernel,
        out_shape=[jax.ShapeDtypeStruct(shape, dtype) for shape, dtype in shapes],
        in_specs=specs,
        out_specs=[pl.BlockSpec(memory_space=pltpu.VMEM) for _ in shapes],
        scratch_shapes=list(scratch),
        name=name,
        cost_estimate=pl.CostEstimate(flops=flops, bytes_accessed=moved, transcendentals=0),
        compiler_params=pltpu.CompilerParams(vmem_limit_bytes=40 * 2**20),
    )(*args)


def everyone(x, axes):
    return lax.all_to_all(x, axes, 0, 0, tiled=True)


def local(mixed, log_decay, beta_logit, conv_weight, norm_gain, out_weight, out_grad):
    chips, groups = lax.axis_size("chip"), lax.axis_size("dp")
    ids = jnp.stack([lax.axis_index("chip"), lax.axis_index("core")]).astype(jnp.int32)
    line = ("chip", "core")
    swap = [(0, 1), (1, 0)]
    width = out_weight.shape[1]

    gates_own = jnp.concatenate([log_decay.T, beta_logit.T, jnp.zeros((4, ROWS), F32)], axis=0)
    other = lax.ppermute(mixed, "core", swap)
    tail = mixed[ROWS - 3 :]
    tail_a = lax.ppermute(tail, line, [(2 * c + 1, 2 * c + 2) for c in range(chips - 1)])
    tail_b = lax.ppermute(tail, line, [(2 * c + 1, 2 * c + 3) for c in range(chips - 1)])
    gates_other = lax.ppermute(gates_own, "core", swap)
    full_grad = lax.all_gather(out_grad, ("core", "dp"), axis=0, tiled=True)

    rows = NB * D
    (padded, pre, q, k, inverse, x, scores, maps, gates, packed) = call(
        maps_kernel,
        [
            ((rows + 8, 3 * D), F32),
            ((rows, 3 * D), F32),
            ((rows, D), F32),
            ((rows, D), F32),
            ((rows, D), F32),
            ((rows, 2 * D), F32),
            ((rows, D), F32),
            ((2 * rows, D), F32),
            ((8, D), F32),
            ((chips, PACK, D), BF16),
        ],
        [ids, mixed, other, tail_a, tail_b, gates_own, gates_other, conv_weight],
        "maps", 10**9, 6 * 10**6,
    )
    gathered = everyone(packed, "chip")
    read, base = call(
        readout_kernel,
        [((2 * rows, D), F32), ((2 * rows, D), F32)],
        [scores, x, q, gates],
        "readout", 10**8, 2 * 10**6, smem=False,
    )
    (back,) = call(
        back_kernel,
        [((rows, D), F32)],
        [ids, full_grad, out_weight],
        "back", 10**8, 2 * 10**6,
    )
    gain = norm_gain.reshape(1, D)
    (states, deltas, grads, reach, packed_grad, normed, sent, gain_part) = call(
        outputs_kernel,
        [
            ((rows, D), F32),
            ((rows, D), F32),
            ((rows, D), F32),
            ((rows, D), F32),
            ((chips, D, D), BF16),
            ((rows, D), BF16),
            ((ROWS, D), BF16),
            ((8, D), F32),
        ],
        [ids, gathered, maps, read, base, gates, back, gain],
        "outputs", 10**9, 6 * 10**6,
    )
    gathered_grad = everyone(packed_grad, "chip")
    received = lax.ppermute(sent, "core", swap)
    dq, dk, pull, row_terms, sums = call(
        local_grads_kernel,
        [
            ((rows, D), F32),
            ((rows, D), F32),
            ((rows, D), F32),
            ((rows, D), F32),
            ((8, D), F32),
        ],
        [scores, deltas, grads, states, q, k, gates],
        "local_grads", 10**9, 4 * 10**6, smem=False,
    )

    height = ROWS // groups
    (share,) = call(
        project_kernel,
        [((groups, height + 16, width), BF16)],
        [ids, normed, received, out_weight, gain_part],
        "project", 10**8, 2 * 10**6,
    )
    shares = everyone(share, "dp").astype(F32)
    result = jnp.sum(shares[:, :height], axis=0).astype(BF16)
    gain_rows = jnp.sum(shares[:, height : height + 2, :D], axis=0)

    weight_part = jnp.einsum("tv,td->vd", normed, full_grad, preferred_element_type=F32)
    weight_parts = everyone(weight_part.astype(BF16).reshape(chips, D // chips, width), "chip")
    weight_sum = jnp.sum(weight_parts.astype(F32), axis=0)
    grad_weight = lax.ppermute(
        weight_sum, line, [(2 * c + h, h * chips + c) for c in range(chips) for h in range(2)]
    )

    keep, send, spill, gate_keep, gate_send, conv_part = call(
        grads_kernel,
        [
            ((ROWS, 4 * D), F32),
            ((ROWS, 4 * D), BF16),
            ((8, 4 * D), F32),
            ((8, ROWS), F32),
            ((8, ROWS), F32),
            ((8, 4 * D), F32),
        ],
        [
            ids, gathered, gathered_grad, maps, reach, states, deltas, inverse, x, q, k, gates,
            pre, padded, dq, dk, pull, row_terms, sums, conv_weight,
        ],
        "grads", 10**9, 8 * 10**6,
        scratch=[pltpu.VMEM((rows + 8, 3 * D), F32)],
    )
    taken = lax.ppermute(send, "core", swap)
    gate_taken = lax.ppermute(gate_send, "core", swap)
    spill_a = lax.ppermute(spill, line, [(2 * c, 2 * c - 1) for c in range(1, chips)])
    spill_b = lax.ppermute(spill, line, [(2 * c + 1, 2 * c - 1) for c in range(1, chips)])

    high = gain_rows[0:1] + gain_rows[1:2]
    gain_high = high.astype(BF16).astype(F32)
    extra = jnp.pad(jnp.concatenate([gain_high, high - gain_high]), ((4, 2), (0, 3 * D)))
    small = (conv_part + extra).astype(BF16)
    smalls = everyone(jnp.broadcast_to(small, (2 * chips, 8, 4 * D)), line)
    totals = jnp.sum(smalls.astype(F32), axis=0)

    spilled = jnp.pad((spill_a + spill_b)[0:3], ((ROWS - 3, 0), (0, 0)))
    grad_mixed = (keep + taken.astype(F32) + spilled).astype(BF16)
    gate_grads = gate_keep + gate_taken
    return (
        result,
        grad_mixed,
        gate_grads[0:2].T,
        gate_grads[2:4].T,
        totals[0:4],
        totals[4, :D] + totals[5, :D],
        grad_weight,
    )


def solution(mesh):
    groups, line = mesh.shape["dp"], mesh.shape["ctx"]
    fine = Mesh(mesh.devices.reshape(groups, line // 2, 2), ("dp", "chip", "core"))
    ctx = ("chip", "core")
    return jax.shard_map(
        local,
        mesh=fine,
        in_specs=(
            P(ctx, "dp"),
            P(ctx, "dp"),
            P(ctx, "dp"),
            P(None, "dp"),
            P(),
            P("dp", None),
            P((*ctx, "dp"), None),
        ),
        out_specs=(
            P((*ctx, "dp"), None),
            P(ctx, "dp"),
            P(ctx, "dp"),
            P(ctx, "dp"),
            P(None, "dp"),
            P(),
            P(("dp", *ctx), None),
        ),
        check_vma=False,
    )
```

```python
import functools
import math

import jax
import jax.numpy as jnp
from jax import lax
from jax.experimental import pallas as pl
from jax.experimental.pallas import tpu as pltpu
from jax.sharding import Mesh
from jax.sharding import PartitionSpec as P

D = 128
ROWS = 256
NB = 4
EPS = 1e-06
SCALE = 1.0 / math.sqrt(D)
HIGHEST = lax.Precision.HIGHEST
F32 = jnp.float32
BF16 = jnp.bfloat16
PACK = 272

FORMS = {
    "nn": (((1,), (0,)), ((), ())),
    "nt": (((1,), (1,)), ((), ())),
    "tn": (((0,), (0,)), ((), ())),
}


def halves(x):
    high = x.astype(BF16)
    return high, (x - high.astype(F32)).astype(BF16)


def mm(a, b, form="nn", passes=1):
    dims = FORMS[form]
    dot = functools.partial(lax.dot_general, dimension_numbers=dims, preferred_element_type=F32)
    if passes == 6:
        return dot(a, b, precision=HIGHEST)
    if passes == 1:
        return dot(a.astype(BF16), b.astype(BF16))
    ah, al = halves(a)
    bh, bl = halves(b)
    return dot(ah, bh) + (dot(ah, bl) + dot(al, bh))


P_KK = 3
P_INV = 3
P_TY = 3
P_MAP = 1
P_OUT = 1
P_BACK = 1


class Taken:
    def __init__(self, source, buffer, sem):
        self.buffer, self.shape, self.waiting = buffer, buffer.shape, True
        self.copy = pltpu.make_async_copy(source, buffer, sem)
        self.copy.start()

    def ready(self):
        if self.waiting:
            self.copy.wait()
            self.waiting = False
        return self

    def __getitem__(self, at):
        return self.ready().buffer[at]


class Given:
    def __init__(self, target, buffer, sem):
        self.buffer, self.shape, self.waiting = buffer, buffer.shape, False
        self.copy = pltpu.make_async_copy(buffer, target, sem)

    def __getitem__(self, at):
        return self.buffer[at]

    def __setitem__(self, at, value):
        self.buffer[at] = value

    def clear(self):
        self.buffer[...] = jnp.zeros_like(self.buffer)

    def whole(self):
        self.copy.start()
        self.waiting = True


def staged(kernel, taken, unread, given, with_ids):
    def body(*refs):
        ids, refs = (refs[:1], refs[1:]) if with_ids else ((), refs)
        sources, refs = refs[:taken], refs[taken + unread :]
        targets, refs = refs[:given], refs[given:]
        in_buffers, refs = refs[:taken], refs[taken:]
        out_buffers, refs = refs[:given], refs[given:]
        in_sems, out_sems, *rest = refs
        ins = [Taken(s, b, in_sems.at[n]) for n, (s, b) in enumerate(zip(sources, in_buffers))]
        outs = [Given(t, b, out_sems.at[n]) for n, (t, b) in enumerate(zip(targets, out_buffers))]
        kernel(*ids, *ins, *outs, *rest)
        for each in ins:
            each.ready()
        for each in outs:
            if not each.waiting:
                each.whole()
        for each in outs:
            each.copy.wait()

    return body


def grid_index():
    return (
        lax.broadcasted_iota(jnp.int32, (D, D), 0),
        lax.broadcasted_iota(jnp.int32, (D, D), 1),
    )


def row_sum(x):
    return jnp.sum(x, axis=-1, keepdims=True)


def triangle_inverses(lowers):
    i, j = grid_index()
    eye = (i == j).astype(F32)
    small = [jnp.where((i >> 3) == (j >> 3), low, 0.0) for low in lowers]
    squares = [mm(s, s, passes=P_INV) for s in small]
    cubes = [mm(s, q, passes=P_INV) for s, q in zip(small, squares)]
    fourths = [mm(q, q, passes=P_INV) for q in squares]
    starts = [eye - s + q - c for s, q, c in zip(small, squares, cubes)]
    inverses = [t + mm(t, f, passes=P_INV) for t, f in zip(starts, fourths)]
    for level in (3, 4, 5, 6):
        joint = ((i >> (level + 1)) == (j >> (level + 1))) & ((i >> level) > (j >> level))
        inner = [
            mm(jnp.where(joint, low, 0.0), t, passes=P_INV) for low, t in zip(lowers, inverses)
        ]
        inverses = [t - mm(t, c, passes=P_INV) for t, c in zip(inverses, inner)]
    return inverses


def silu(u):
    return u / (1.0 + jnp.exp(-u))


def unit(raw):
    inverse = lax.rsqrt(row_sum(raw * raw) + EPS)
    return raw * inverse, inverse


def block(b):
    return slice(b * D, (b + 1) * D)


def value_lanes(core):
    return pl.ds(pl.multiple_of(2 * D + core * D, D), D)


def lane_groups(core):
    return (slice(0, D), slice(D, 2 * D), value_lanes(core))


def damping(cum_col, cum_row):
    i, j = grid_index()
    causal = i >= j
    return jnp.where(causal, jnp.exp(jnp.where(causal, cum_col - cum_row, 0.0)), 0.0)


def gate_columns(gates):
    return jnp.transpose(gates)


def maps_kernel(
    ids, mixed, other, tail_a, tail_b, gate_own, gate_other, conv_w,
    padded, pre, q_out, k_out, inverse_out, x_out, scores_out, maps_out, gates_out, packed,
):
    core = ids[1]
    for group, lanes in enumerate(lane_groups(core)):
        here = slice(group * D, (group + 1) * D)
        padded[0:8, here] = jnp.zeros((8, D), F32)
        tail = tail_a[:, lanes].astype(F32) + tail_b[:, lanes].astype(F32)
        padded[5:8, here] = tail[13:16]
        padded[pl.ds(8 + core * ROWS, ROWS), here] = mixed[:, lanes].astype(F32)
        padded[pl.ds(8 + (1 - core) * ROWS, ROWS), here] = other[:, lanes].astype(F32)

    gates_out.clear()
    for source, own in ((gate_own, True), (gate_other, False)):
        picked = jnp.where(core == 0, source[...], pltpu.roll(source[...], 7, 0))
        at = (core if own else 1 - core) * 2
        for half in range(2):
            gates_out[pl.ds(at + half, 1), :] = picked[0:1, block(half)]
            gates_out[pl.ds(4 + at + half, 1), :] = picked[2:3, block(half)]
    i, j = grid_index()
    raw = gates_out[...]
    upto = (i <= j).astype(F32)
    cumulative = mm(raw, upto, passes=6)
    is_decay = lax.broadcasted_iota(jnp.int32, (8, D), 0) < 4
    gates = jnp.where(is_decay, cumulative, 1.0 / (1.0 + jnp.exp(-raw)))
    gates_out[...] = gates
    columns = gate_columns(gates)

    qs, ks, vs = [], [], []
    for b in range(NB):
        pieces = []
        for group, lanes in enumerate(lane_groups(core)):
            here = slice(group * D, (group + 1) * D)
            total = conv_w[0:1, lanes] * padded[5 + b * D : 5 + (b + 1) * D, here]
            for tap in range(1, 4):
                start = 5 + tap + b * D
                total = total + conv_w[tap : tap + 1, lanes] * padded[start : start + D, here]
            pre[block(b), here] = total
            pieces.append(silu(total).astype(BF16).astype(F32))
        q = unit(pieces[0])[0] * SCALE
        k = unit(pieces[1])[0]
        q_out[block(b), :] = q
        k_out[block(b), :] = k
        qs.append(q)
        ks.append(k)
        vs.append(pieces[2])
    for each in (padded, pre, q_out, k_out, gates_out):
        each.whole()

    strict = i > j
    lowers = []
    for b in range(NB):
        damp = damping(columns[:, b : b + 1], gates[b : b + 1, :])
        both = mm(jnp.concatenate([ks[b], qs[b]], axis=0), ks[b], "nt", P_KK)
        lowers.append(jnp.where(strict, columns[:, 4 + b : 5 + b] * damp * both[0:D], 0.0))
        scores_out[block(b), :] = damp * both[D:]
    scores_out.whole()
    inverses = triangle_inverses(lowers)
    maps, decays = [], []
    for b in range(NB):
        inverse_out[block(b), :] = inverses[b]
        cum, beta = columns[:, b : b + 1], columns[:, 4 + b : 5 + b]
        stacked = jnp.concatenate([(beta * jnp.exp(cum)) * ks[b], beta * vs[b]], axis=1)
        x = mm(inverses[b], stacked, passes=P_TY)
        x_out[block(b), :] = x
        end = gates[b : b + 1, D - 1 : D]
        tail_keys = jnp.exp(end - cum) * ks[b]
        both = mm(x, tail_keys, "tn", P_MAP)
        maps_out[2 * b * D : 2 * (b + 1) * D, :] = both
        maps.append(both)
        decays.append(jnp.exp(end))
    for each in (inverse_out, x_out, maps_out):
        each.whole()

    def compose(first, first_decay, then, then_decay):
        moved = mm(first, then[0:D], passes=P_MAP)
        through = then_decay * first[0:D] + first_decay * then[0:D] - moved[0:D]
        added = then_decay * first[D:] - moved[D:] + then[D:]
        return jnp.concatenate([through, added], axis=0), first_decay * then_decay

    early, early_decay = compose(maps[0], decays[0], maps[1], decays[1])
    late, late_decay = compose(maps[2], decays[2], maps[3], decays[3])
    whole, decay = compose(early, early_decay, late, late_decay)
    whole = whole.astype(BF16)
    row = lax.broadcasted_iota(jnp.int32, (16, D), 0)
    decay = jnp.broadcast_to(decay, (16, D))
    high = decay.astype(BF16).astype(F32)
    low = (decay - high).astype(BF16).astype(F32)
    lowest = decay - high - low
    parts = jnp.where(row == 0, high, jnp.where(row == 1, low, jnp.where(row == 2, lowest, 0.0)))
    parts = parts.astype(BF16)
    for copy in range(packed.shape[0]):
        packed[copy, 0 : 2 * D, :] = whole
        packed[copy, 2 * D : PACK, :] = parts


def readout_kernel(scores, x, q, gates, read_out, base_out):
    columns = gate_columns(gates[...])
    for b in range(NB):
        px = mm(scores[block(b), :], x[block(b), :], passes=P_TY)
        grown = jnp.exp(columns[:, b : b + 1]) * q[block(b), :]
        read_out[2 * b * D : (2 * b + 1) * D, :] = grown - px[:, 0:D]
        read_out[(2 * b + 1) * D : 2 * (b + 1) * D, :] = -x[block(b), 0:D]
        base_out[2 * b * D : (2 * b + 1) * D, :] = px[:, D:]
        base_out[(2 * b + 1) * D : 2 * (b + 1) * D, :] = x[block(b), D:]


def back_kernel(ids, grad_own, grad_other, weight, back_out):
    core = ids[1]
    weight.ready()
    head = weight[pl.ds(pl.multiple_of(core * D, D), D), :]
    back_out[pl.ds(pl.multiple_of(core * ROWS, ROWS), ROWS), :] = mm(grad_own[...], head, "nt")
    back_out[pl.ds(pl.multiple_of((1 - core) * ROWS, ROWS), ROWS), :] = mm(
        grad_other[...], head, "nt"
    )


def slab_decay(piece):
    return jnp.sum(piece[2 * D : PACK].astype(F32), axis=0, keepdims=True)


def forward_fold(gathered, first, last, state):
    def step(position, state):
        piece = gathered[position]
        return slab_decay(piece) * state + (
            piece[D : 2 * D].astype(F32) - mm(state, piece[0:D], passes=P_MAP)
        )

    return lax.fori_loop(first, last, step, state)


def backward_fold(gathered, gathered_grad, first, last, total):
    def step(count, total):
        position = last - 1 - count
        piece = gathered[position]
        return slab_decay(piece) * total + (
            gathered_grad[position].astype(F32) - mm(total, piece[0:D], "nt", P_MAP)
        )

    return lax.fori_loop(0, last - first, step, total)


def forward_total_kernel(gathered, out):
    gathered.ready()
    out[...] = forward_fold(gathered, 0, gathered.shape[0], jnp.zeros((D, D), F32))


def backward_total_kernel(gathered, gathered_grad, out):
    gathered.ready()
    gathered_grad.ready()
    count = gathered.shape[0]
    out[...] = backward_fold(gathered, gathered_grad, 0, count, jnp.zeros((D, D), F32))


def outputs_kernel(
    ids, gathered, entry, maps, read, base, gates, back, gain,
    states_out, deltas_out, grads_out, reach_out, packed_grad, normed_out, sent, gain_out,
):
    chip, core = ids[0], ids[1]
    gathered.ready()
    state = forward_fold(gathered, 0, chip, entry[...])
    states, decays = [], []
    for b in range(NB):
        states.append(state)
        states_out[block(b), :] = state
        decay = jnp.exp(gates[b : b + 1, D - 1 : D])
        decays.append(decay)
        if b + 1 < NB:
            here = maps[2 * b * D : 2 * (b + 1) * D, :]
            state = decay * state - mm(state, here[0:D], passes=P_MAP) + here[D:]
    total_gain = jnp.zeros((1, D), F32)
    reaches = []
    for b in range(NB):
        both = slice(2 * b * D, 2 * (b + 1) * D)
        rows = base[both, :] + mm(read[both, :], states[b], "nt", P_OUT)
        out = rows[0:D]
        deltas_out[block(b), :] = rows[D:]
        inverse = lax.rsqrt(row_sum(out * out) * (1.0 / D) + EPS)
        unit_out = out * inverse
        normed = (unit_out * gain[0:1, :]).astype(BF16)
        normed_out[block(b), :] = normed

        @pl.when((b // 2) != core)
        def _():
            sent[block(b % 2), :] = normed

        cotangent = back[block(b), :]
        total_gain = total_gain + jnp.sum(cotangent * unit_out, axis=0, keepdims=True)
        scaled = cotangent * gain[0:1, :]
        grad = inverse * (scaled - unit_out * (row_sum(scaled * unit_out) * (1.0 / D)))
        grads_out[block(b), :] = grad
        reach = mm(grad, read[2 * b * D : (2 * b + 1) * D, :], "tn", P_OUT)
        reach_out[block(b), :] = reach
        reaches.append(reach)
    for each in (states_out, deltas_out, grads_out, reach_out, normed_out, sent):
        each.whole()
    gain_out[...] = jnp.broadcast_to(total_gain, (8, D))
    state_grad = reaches[NB - 1]
    for b in range(NB - 2, -1, -1):
        through = maps[2 * b * D : (2 * b + 1) * D, :]
        state_grad = decays[b] * state_grad - mm(state_grad, through, "nt", P_MAP) + reaches[b]
    state_grad = state_grad.astype(BF16)
    for copy in range(packed_grad.shape[0]):
        packed_grad[copy] = state_grad


def local_grads_kernel(
    scores, deltas, grads, states, q, k, gates,
    dq_out, dk_out, pull_out, rows_out, sums_out,
):
    columns = gate_columns(gates[...])
    i, j = grid_index()
    sums_out.clear()
    for b in range(NB):
        at = block(b)
        grad, score = grads[at, :], scores[at, :]
        damp = damping(columns[:, b : b + 1], gates[b : b + 1, :])
        d_score = jnp.where(i >= j, mm(grad, deltas[at, :], "nt", P_BACK), 0.0)
        d_inner = d_score * damp
        sums_out[b : b + 1, :] = jnp.sum(d_score * score, axis=0, keepdims=True)
        reading = mm(grad, states[at, :], passes=P_BACK)
        growth = jnp.exp(columns[:, b : b + 1])
        dq_out[at, :] = growth * reading + mm(d_inner, k[at, :], passes=P_BACK)
        dk_out[at, :] = mm(d_inner, q[at, :], "tn", P_BACK)
        pull_out[at, :] = mm(score, grad, "tn", P_BACK)
        row = row_sum(d_score * score) + row_sum(growth * q[at, :] * reading)
        rows_out[at, :] = jnp.broadcast_to(row, (D, D))


def grads_kernel(
    ids, gathered, gathered_grad, leaving, maps, reach, states, deltas, inverse, x, q, k, gates, pre, padded,
    dq, dk, pull, rows_in, sums, conv_w,
    keep_out, send_out, spill_out, gate_keep, gate_send, conv_out,
    d_pre,
):
    chip, core = ids[0], ids[1]
    gathered.ready()
    gathered_grad.ready()
    exit_grad = backward_fold(
        gathered, gathered_grad, chip + 1, gathered.shape[0], leaving[...]
    )
    columns = gate_columns(gates[...])
    i, j = grid_index()
    strict = i > j
    exits = [None] * NB
    decays = [jnp.exp(gates[b : b + 1, D - 1 : D]) for b in range(NB)]
    for b in range(NB - 1, -1, -1):
        exits[b] = exit_grad
        if b:
            through = maps[2 * b * D : (2 * b + 1) * D, :]
            exit_grad = (
                decays[b] * exit_grad - mm(exit_grad, through, "nt", P_MAP) + reach[block(b), :]
            )
    d_pre[NB * D : NB * D + 8, :] = jnp.zeros((8, 3 * D), F32)
    lane = lax.broadcasted_iota(jnp.int32, (D, D), 1)
    row_terms = jnp.zeros((D, D), F32)
    beta_terms = jnp.zeros((D, D), F32)
    col_rows, end_rows = [], []
    for b in range(NB):
        at = block(b)
        key, query = k[at, :], q[at, :]
        cum, beta = columns[:, b : b + 1], columns[:, 4 + b : 5 + b]
        growth = jnp.exp(cum)
        remain = jnp.exp(gates[b : b + 1, D - 1 : D] - cum)
        damp = damping(cum, gates[b : b + 1, :])
        tail_keys = remain * key
        d_delta = pull[at, :] + mm(tail_keys, exits[b], "nt", P_BACK)
        d_x = jnp.concatenate([-mm(d_delta, states[at, :], passes=P_BACK), d_delta], axis=1)
        d_y = mm(inverse[at, :], d_x, "tn", P_BACK)
        both = x[at, :]
        d_lower = jnp.where(strict, -mm(d_y, both, "nt", P_BACK), 0.0)
        d_inner = d_lower * (beta * damp)
        inner = mm(key, key, "nt", P_KK)
        elementwise = d_inner * inner
        d_tail = mm(deltas[at, :], exits[b], passes=P_BACK)
        symmetric = d_inner + jnp.transpose(d_inner)
        d_key = (
            dk[at, :]
            + mm(symmetric, key, passes=P_BACK)
            + (beta * growth) * d_y[:, 0:D]
            + remain * d_tail
        )
        d_query = dq[at, :]
        tail_dot = row_sum(d_tail * tail_keys)
        written = row_sum((beta * growth) * key * d_y[:, 0:D])
        row = rows_in[at, :] + (row_sum(elementwise) + written - tail_dot)
        row_terms = jnp.where(lane == b, row, row_terms)
        beta_terms = jnp.where(lane == b, (1.0 - beta) * row_sum(d_y * both), beta_terms)
        col_rows.append(sums[b : b + 1, :] + jnp.sum(elementwise, axis=0, keepdims=True))
        end = jnp.sum(tail_dot, axis=0, keepdims=True) + decays[b] * jnp.sum(
            row_sum(exits[b] * states[at, :]), axis=0, keepdims=True
        )
        end_rows.append(jnp.broadcast_to(end, (1, D)))

        u_q, u_k, u_v = pre[at, 0:D], pre[at, D : 2 * D], pre[at, 2 * D :]
        sigmoids = [1.0 / (1.0 + jnp.exp(-u)) for u in (u_q, u_k, u_v)]
        raw_q = (u_q * sigmoids[0]).astype(BF16).astype(F32)
        raw_k = (u_k * sigmoids[1]).astype(BF16).astype(F32)
        unit_q, inverse_q = unit(raw_q)
        inverse_k = unit(raw_k)[1]
        d_unit = d_query * SCALE
        d_raw_q = inverse_q * (d_unit - unit_q * row_sum(unit_q * d_unit))
        d_raw_k = inverse_k * (d_key - key * row_sum(key * d_key))
        d_raw_v = beta * d_y[:, D:]
        for group, (d_raw, u, s) in enumerate(
            zip((d_raw_q, d_raw_k, d_raw_v), (u_q, u_k, u_v), sigmoids)
        ):
            d_pre[at, group * D : (group + 1) * D] = d_raw * (s * (1.0 + u * (1.0 - s)))

    rows = jnp.transpose(row_terms)[0:8, :] - jnp.concatenate(
        col_rows + [jnp.zeros((4, D), F32)], axis=0
    )
    d_decay = mm(rows, (i >= j).astype(F32), passes=6) + jnp.concatenate(
        end_rows + [jnp.zeros((4, D), F32)], axis=0
    )
    d_logit = jnp.transpose(beta_terms)[0:8, :]
    for target, own in ((gate_keep, True), (gate_send, False)):
        target.clear()
        for head in range(2):

            @pl.when(core == head)
            def _():
                first = 2 * (head if own else 1 - head)
                for half in range(2):
                    b = first + half
                    target[head : head + 1, block(half)] = d_decay[b : b + 1, :]
                    target[2 + head : 3 + head, block(half)] = d_logit[b : b + 1, :]

    keep_out.clear()
    send_out.clear()
    spill_out.clear()
    conv_out.clear()
    for group, lanes in enumerate(lane_groups(core)):
        here = slice(group * D, (group + 1) * D)
        taps = [conv_w[tap : tap + 1, lanes] for tap in range(4)]
        sums_of = [jnp.zeros((1, D), F32) for _ in range(4)]
        for b in range(NB):
            total = taps[3] * d_pre[b * D : (b + 1) * D, here]
            for tap in range(3):
                start = b * D + 3 - tap
                total = total + taps[tap] * d_pre[start : start + D, here]
            mine = (b // 2) == core
            at = slice((b % 2) * D, (b % 2 + 1) * D)

            @pl.when(mine)
            def _():
                keep_out[at, lanes] = total

            @pl.when(jnp.logical_not(mine))
            def _():
                send_out[at, lanes] = total.astype(BF16)

            for tap in range(4):
                start = 5 + tap + b * D
                sums_of[tap] = sums_of[tap] + jnp.sum(
                    d_pre[b * D : (b + 1) * D, here] * padded[start : start + D, here],
                    axis=0,
                    keepdims=True,
                )
        for tap in range(4):
            conv_out[tap : tap + 1, lanes] = sums_of[tap]
        for back in range(1, 4):
            total = jnp.zeros((1, D), F32)
            for tap in range(0, 4 - back):
                at = 3 - back - tap
                total = total + taps[tap] * d_pre[at : at + 1, here]
            spill_out[3 - back : 4 - back, lanes] = total


def shares_kernel(ids, normed, received, weight, gain_part, grad_own, grad_other, out, weight_out):
    core = ids[1]
    normed.ready()
    weight.ready()
    kept = normed[pl.ds(pl.multiple_of(core * ROWS, ROWS), ROWS), :]
    given = normed[pl.ds(pl.multiple_of((1 - core) * ROWS, ROWS), ROWS), :]
    mine = weight[pl.ds(pl.multiple_of(core * D, D), D), :]
    others = weight[pl.ds(pl.multiple_of((1 - core) * D, D), D), :]
    share = (mm(kept, mine) + mm(received[...], others)).astype(BF16)
    count, height = out.shape[0], out.shape[1] - 16
    row = lax.broadcasted_iota(jnp.int32, (16, D), 0)
    gain = jnp.broadcast_to(gain_part[0:1, :], (16, D))
    high = gain.astype(BF16).astype(F32)
    extra = jnp.where(row == 0, high, jnp.where(row == 1, gain - high, 0.0)).astype(BF16)
    for owner in range(count):
        out[owner, 0:height, :] = share[owner * height : (owner + 1) * height]
        out[owner, height:, :] = jnp.zeros((16, out.shape[2]), BF16)
        out[owner, height:, 0:D] = extra
    out.whole()
    weight_out[...] = (mm(kept, grad_own[...], "tn") + mm(given, grad_other[...], "tn")).astype(BF16)


def call(kernel, shapes, args, name, flops, scratch=(), with_ids=True, after=()):
    arrays = args[1:] if with_ids else args
    outs = [jax.ShapeDtypeStruct(shape, dtype) for shape, dtype in shapes]
    anywhere = pl.BlockSpec(memory_space=pl.ANY)
    moved = sum(x.size * x.dtype.itemsize for x in [*arrays, *outs])
    return pl.pallas_call(
        staged(kernel, len(arrays), len(after), len(outs), with_ids),
        out_shape=outs,
        in_specs=[pl.BlockSpec(memory_space=pltpu.SMEM)] * with_ids
        + [anywhere] * (len(arrays) + len(after)),
        out_specs=[anywhere] * len(outs),
        scratch_shapes=[
            *[pltpu.VMEM(x.shape, x.dtype) for x in [*arrays, *outs]],
            pltpu.SemaphoreType.DMA((len(arrays),)),
            pltpu.SemaphoreType.DMA((len(outs),)),
            *scratch,
        ],
        name=name,
        cost_estimate=pl.CostEstimate(flops=flops, bytes_accessed=moved, transcendentals=0),
    )(*args, *after)


def everyone(x, axes):
    return lax.all_to_all(x, axes, 0, 0, tiled=True)


def local(mixed, log_decay, beta_logit, conv_weight, norm_gain, out_weight, out_grad):
    near, groups = lax.axis_size("near"), lax.axis_size("dp")
    chips = lax.axis_size("far") * near
    ids = jnp.stack([lax.axis_index(axis) for axis in ("near", "core")]).astype(jnp.int32)
    chip_line, line = ("far", "near"), ("far", "near", "core")
    swap = [(0, 1), (1, 0)]
    width = out_weight.shape[1]
    rows = NB * D
    height = ROWS // groups

    gates_own = jnp.concatenate([log_decay.T, beta_logit.T, jnp.zeros((4, ROWS), F32)], axis=0)
    tail = mixed[ROWS - 16 :]
    tail_a = lax.ppermute(tail, line, [(2 * c + 1, 2 * c + 2) for c in range(chips - 1)])
    tail_b = lax.ppermute(tail, line, [(2 * c + 1, 2 * c + 3) for c in range(chips - 1)])
    other = lax.ppermute(mixed, "core", swap)
    gates_other = lax.ppermute(gates_own, "core", swap)
    out_grad, gates_other, tail_a, tail_b, other = lax.optimization_barrier(
        (out_grad, gates_other, tail_a, tail_b, other)
    )
    grad_own = everyone(jnp.broadcast_to(out_grad[None], (groups, height, width)), "dp")
    grad_own = grad_own.reshape(ROWS, width)
    (padded, pre, q, k, inverse, x, scores, maps, gates, packed) = call(
        maps_kernel,
        [
            ((rows + 8, 3 * D), F32),
            ((rows, 3 * D), F32),
            ((rows, D), F32),
            ((rows, D), F32),
            ((rows, D), F32),
            ((rows, 2 * D), F32),
            ((rows, D), F32),
            ((2 * rows, D), F32),
            ((8, D), F32),
            ((near, PACK, D), BF16),
        ],
        [ids, mixed, other, tail_a, tail_b, gates_own, gates_other, conv_weight],
        "maps", 10**9,
    )
    gathered = everyone(packed, "near")

    grad_other = lax.ppermute(grad_own, "core", swap)
    read, base = call(
        readout_kernel,
        [((2 * rows, D), F32), ((2 * rows, D), F32)],
        [scores, x, q, gates],
        "readout", 10**8, with_ids=False,
    )
    (back,) = call(
        back_kernel,
        [((rows, D), F32)],
        [ids, grad_own, grad_other, out_weight],
        "back", 10**8,
    )
    (total,) = call(
        forward_total_kernel,
        [((D, D), F32)],
        [gathered],
        "forward_total", 10**8, with_ids=False, after=[read, back],
    )
    entry = lax.ppermute(total, "far", [(0, 1)])
    gain = jnp.broadcast_to(norm_gain.reshape(1, D), (8, D))
    (states, deltas, grads, reach, packed_grad, normed, sent, gain_part) = call(
        outputs_kernel,
        [
            ((rows, D), F32),
            ((rows, D), F32),
            ((rows, D), F32),
            ((rows, D), F32),
            ((near, D, D), BF16),
            ((rows, D), BF16),
            ((ROWS, D), BF16),
            ((8, D), F32),
        ],
        [ids, gathered, entry, maps, read, base, gates, back, gain],
        "outputs", 10**9,
    )
    gathered_grad = everyone(packed_grad, "near")
    received = lax.ppermute(sent, "core", swap)
    dq, dk, pull, row_terms, sums = call(
        local_grads_kernel,
        [
            ((rows, D), F32),
            ((rows, D), F32),
            ((rows, D), F32),
            ((rows, D), F32),
            ((8, D), F32),
        ],
        [scores, deltas, grads, states, q, k, gates],
        "local_grads", 10**9, with_ids=False,
    )
    share, weight_part = call(
        shares_kernel,
        [((groups, height + 16, width), BF16), ((D, width), BF16)],
        [ids, normed, received, out_weight, gain_part, grad_own, grad_other],
        "shares", 10**8, after=[sums],
    )

    (total,) = call(
        backward_total_kernel,
        [((D, D), F32)],
        [gathered, gathered_grad],
        "backward_total", 10**8, with_ids=False,
    )
    total, share = lax.optimization_barrier((total, share))
    leaving = lax.ppermute(total, "far", [(1, 0)])
    keep, send, spill, gate_keep, gate_send, conv_part = call(
        grads_kernel,
        [
            ((ROWS, 4 * D), F32),
            ((ROWS, 4 * D), BF16),
            ((8, 4 * D), F32),
            ((8, ROWS), F32),
            ((8, ROWS), F32),
            ((8, 4 * D), F32),
        ],
        [
            ids, gathered, gathered_grad, leaving, maps, reach, states, deltas, inverse, x, q, k, gates,
            pre, padded, dq, dk, pull, row_terms, sums, conv_weight,
        ],
        "grads", 10**9,
        scratch=[pltpu.VMEM((rows + 8, 3 * D), F32)],
    )
    shares = everyone(share, "dp").astype(F32)
    result = jnp.sum(shares[:, :height], axis=0).astype(BF16)
    gain_rows = jnp.sum(shares[:, height : height + 2, :D], axis=0)

    gain_row = gain_rows[0:1] + gain_rows[1:2]
    totals = conv_part + jnp.pad(gain_row, ((4, 3), (0, 3 * D)))
    totals = totals + lax.ppermute(totals, "core", swap)
    totals, send, spill, gate_send, weight_part = lax.optimization_barrier(
        (totals, send, spill, gate_send, weight_part)
    )
    taken = lax.ppermute(send, "core", swap)
    gate_taken = lax.ppermute(gate_send, "core", swap)
    spill_a = lax.ppermute(spill, line, [(2 * c, 2 * c - 1) for c in range(1, chips)])
    spill_b = lax.ppermute(spill, line, [(2 * c + 1, 2 * c - 1) for c in range(1, chips)])
    distance = 1
    while distance < chips:
        pairs = [(c, c ^ distance) for c in range(chips)]
        seen = lax.ppermute(totals, chip_line, pairs)
        last = distance * 2 == chips
        if not last:
            totals = totals + seen
        distance *= 2
    grad_taps = totals[0:4] + seen[0:4]
    grad_gain = totals[4, :D] + seen[4, :D]

    weight_parts = everyone(weight_part.reshape(chips, D // chips, width), chip_line)
    weight_sum = jnp.sum(weight_parts.astype(F32), axis=0)
    grad_weight = lax.ppermute(
        weight_sum, line, [(2 * c + h, h * chips + c) for c in range(chips) for h in range(2)]
    )

    spilled = jnp.pad((spill_a + spill_b)[0:3], ((ROWS - 3, 0), (0, 0)))
    grad_mixed = (keep + taken.astype(F32) + spilled).astype(BF16)
    gate_grads = gate_keep + gate_taken
    return (
        result,
        grad_mixed,
        gate_grads[0:2].T,
        gate_grads[2:4].T,
        grad_taps,
        grad_gain,
        grad_weight,
    )


def solution(mesh):
    groups, line = mesh.shape["dp"], mesh.shape["ctx"]
    ctx = ("far", "near", "core")
    fine = Mesh(mesh.devices.reshape(groups, 2, line // 4, 2), ("dp", *ctx))
    return jax.shard_map(
        local,
        mesh=fine,
        in_specs=(
            P(ctx, "dp"),
            P(ctx, "dp"),
            P(ctx, "dp"),
            P(None, "dp"),
            P(),
            P("dp", None),
            P((*ctx, "dp"), None),
        ),
        out_specs=(
            P((*ctx, "dp"), None),
            P(ctx, "dp"),
            P(ctx, "dp"),
            P(ctx, "dp"),
            P(None, "dp"),
            P(),
            P(("dp", *ctx), None),
        ),
        check_vma=False,
    )
```

```python
import functools
import math

import jax
import jax.numpy as jnp
from jax import lax
from jax.experimental import pallas as pl
from jax.experimental.pallas import tpu as pltpu
from jax.sharding import Mesh
from jax.sharding import PartitionSpec as P

D = 128
ROWS = 256
NB = 4
EPS = 1e-06
SCALE = 1.0 / math.sqrt(D)
HIGHEST = lax.Precision.HIGHEST
F32 = jnp.float32
BF16 = jnp.bfloat16
PACK = 272

FORMS = {
    "nn": (((1,), (0,)), ((), ())),
    "nt": (((1,), (1,)), ((), ())),
    "tn": (((0,), (0,)), ((), ())),
}


def halves(x):
    high = x.astype(BF16)
    return high, (x - high.astype(F32)).astype(BF16)


def mm(a, b, form="nn", passes=1):
    dims = FORMS[form]
    dot = functools.partial(lax.dot_general, dimension_numbers=dims, preferred_element_type=F32)
    if passes == 6:
        return dot(a, b, precision=HIGHEST)
    if passes == 1:
        return dot(a.astype(BF16), b.astype(BF16))
    ah, al = halves(a)
    bh, bl = halves(b)
    return dot(ah, bh) + (dot(ah, bl) + dot(al, bh))


P_KK = 3
P_INV = 3
P_TY = 3
P_MAP = 1
P_OUT = 1
P_BACK = 1


class Taken:
    def __init__(self, source, buffer, sem):
        self.buffer, self.shape, self.waiting = buffer, buffer.shape, True
        self.copy = pltpu.make_async_copy(source, buffer, sem)
        self.copy.start()

    def ready(self):
        if self.waiting:
            self.copy.wait()
            self.waiting = False
        return self

    def __getitem__(self, at):
        return self.ready().buffer[at]


class Given:
    def __init__(self, target, buffer, sem):
        self.buffer, self.shape, self.waiting = buffer, buffer.shape, False
        self.copy = pltpu.make_async_copy(buffer, target, sem)

    def __getitem__(self, at):
        return self.buffer[at]

    def __setitem__(self, at, value):
        self.buffer[at] = value

    def clear(self):
        self.buffer[...] = jnp.zeros_like(self.buffer)

    def whole(self):
        self.copy.start()
        self.waiting = True


class Resident:
    def __init__(self, buffer):
        self.buffer, self.shape = buffer, buffer.shape

    def ready(self):
        return self

    def __getitem__(self, at):
        return self.buffer[at]

    def __setitem__(self, at, value):
        self.buffer[at] = value

    def clear(self):
        self.buffer[...] = jnp.zeros_like(self.buffer)

    def whole(self):
        pass


def staged(kernel, inputs, unread, outputs, with_ids):
    def body(*refs):
        ids, refs = (refs[:1], refs[1:]) if with_ids else ((), refs)
        sources, refs = refs[: len(inputs)], refs[len(inputs) + unread :]
        targets, refs = refs[: len(outputs)], refs[len(outputs) :]
        moved_in, moved_out = inputs.count(False), outputs.count(False)
        in_buffers, refs = list(refs[:moved_in]), refs[moved_in:]
        out_buffers, refs = list(refs[:moved_out]), refs[moved_out:]
        in_sems, out_sems, *rest = refs
        ins, outs, waits = [], [], []
        for source, resident in zip(sources, inputs):
            sem = in_sems.at[moved_in - len(in_buffers)]
            ins.append(Resident(source) if resident else Taken(source, in_buffers.pop(0), sem))
        for target, resident in zip(targets, outputs):
            if resident:
                outs.append(Resident(target))
            else:
                sem = out_sems.at[moved_out - len(out_buffers)]
                outs.append(Given(target, out_buffers.pop(0), sem))
                waits.append(outs[-1])
        kernel(*ids, *ins, *outs, *rest)
        for each in ins:
            each.ready()
        for each in waits:
            if not each.waiting:
                each.whole()
        for each in waits:
            each.copy.wait()

    return body


def grid_index():
    return (
        lax.broadcasted_iota(jnp.int32, (D, D), 0),
        lax.broadcasted_iota(jnp.int32, (D, D), 1),
    )


def row_sum(x):
    return jnp.sum(x, axis=-1, keepdims=True)


def triangle_inverses(lowers):
    i, j = grid_index()
    eye = (i == j).astype(F32)
    small = [jnp.where((i >> 3) == (j >> 3), low, 0.0) for low in lowers]
    squares = [mm(s, s, passes=P_INV) for s in small]
    cubes = [mm(s, q, passes=P_INV) for s, q in zip(small, squares)]
    fourths = [mm(q, q, passes=P_INV) for q in squares]
    starts = [eye - s + q - c for s, q, c in zip(small, squares, cubes)]
    inverses = [t + mm(t, f, passes=P_INV) for t, f in zip(starts, fourths)]
    for level in (3, 4, 5, 6):
        joint = ((i >> (level + 1)) == (j >> (level + 1))) & ((i >> level) > (j >> level))
        inner = [
            mm(jnp.where(joint, low, 0.0), t, passes=P_INV) for low, t in zip(lowers, inverses)
        ]
        inverses = [t - mm(t, c, passes=P_INV) for t, c in zip(inverses, inner)]
    return inverses


def silu(u):
    return u / (1.0 + jnp.exp(-u))


def unit(raw):
    inverse = lax.rsqrt(row_sum(raw * raw) + EPS)
    return raw * inverse, inverse


def block(b):
    return slice(b * D, (b + 1) * D)


def value_lanes(core):
    return pl.ds(pl.multiple_of(2 * D + core * D, D), D)


def lane_groups(core):
    return (slice(0, D), slice(D, 2 * D), value_lanes(core))


def damping(cum_col, cum_row):
    i, j = grid_index()
    causal = i >= j
    return jnp.where(causal, jnp.exp(jnp.where(causal, cum_col - cum_row, 0.0)), 0.0)


def gate_columns(gates):
    return jnp.transpose(gates)


def maps_kernel(
    ids, mixed, other, tail_a, tail_b, gate_own, gate_other, conv_w,
    padded, pre, q_out, k_out, inverse_out, x_out, scores_out, maps_out, gates_out, packed,
):
    core = ids[1]
    for group, lanes in enumerate(lane_groups(core)):
        here = slice(group * D, (group + 1) * D)
        padded[0:8, here] = jnp.zeros((8, D), F32)
        tail = tail_a[:, lanes].astype(F32) + tail_b[:, lanes].astype(F32)
        padded[5:8, here] = tail[13:16]
        padded[pl.ds(8 + core * ROWS, ROWS), here] = mixed[:, lanes].astype(F32)
        padded[pl.ds(8 + (1 - core) * ROWS, ROWS), here] = other[:, lanes].astype(F32)

    gates_out.clear()
    for source, own in ((gate_own, True), (gate_other, False)):
        picked = jnp.where(core == 0, source[...], pltpu.roll(source[...], 7, 0))
        at = (core if own else 1 - core) * 2
        for half in range(2):
            gates_out[pl.ds(at + half, 1), :] = picked[0:1, block(half)]
            gates_out[pl.ds(4 + at + half, 1), :] = picked[2:3, block(half)]
    i, j = grid_index()
    raw = gates_out[...]
    upto = (i <= j).astype(F32)
    cumulative = mm(raw, upto, passes=6)
    is_decay = lax.broadcasted_iota(jnp.int32, (8, D), 0) < 4
    gates = jnp.where(is_decay, cumulative, 1.0 / (1.0 + jnp.exp(-raw)))
    gates_out[...] = gates
    columns = gate_columns(gates)

    qs, ks, vs = [], [], []
    for b in range(NB):
        pieces = []
        for group, lanes in enumerate(lane_groups(core)):
            here = slice(group * D, (group + 1) * D)
            total = conv_w[0:1, lanes] * padded[5 + b * D : 5 + (b + 1) * D, here]
            for tap in range(1, 4):
                start = 5 + tap + b * D
                total = total + conv_w[tap : tap + 1, lanes] * padded[start : start + D, here]
            pre[block(b), here] = total
            pieces.append(silu(total).astype(BF16).astype(F32))
        q = unit(pieces[0])[0] * SCALE
        k = unit(pieces[1])[0]
        q_out[block(b), :] = q
        k_out[block(b), :] = k
        qs.append(q)
        ks.append(k)
        vs.append(pieces[2])
    for each in (padded, pre, q_out, k_out, gates_out):
        each.whole()

    strict = i > j
    lowers = []
    for b in range(NB):
        damp = damping(columns[:, b : b + 1], gates[b : b + 1, :])
        both = mm(jnp.concatenate([ks[b], qs[b]], axis=0), ks[b], "nt", P_KK)
        lowers.append(jnp.where(strict, columns[:, 4 + b : 5 + b] * damp * both[0:D], 0.0))
        scores_out[block(b), :] = damp * both[D:]
    scores_out.whole()
    inverses = triangle_inverses(lowers)
    maps, decays = [], []
    for b in range(NB):
        inverse_out[block(b), :] = inverses[b]
        cum, beta = columns[:, b : b + 1], columns[:, 4 + b : 5 + b]
        stacked = jnp.concatenate([(beta * jnp.exp(cum)) * ks[b], beta * vs[b]], axis=1)
        x = mm(inverses[b], stacked, passes=P_TY)
        x_out[block(b), :] = x
        end = gates[b : b + 1, D - 1 : D]
        tail_keys = jnp.exp(end - cum) * ks[b]
        both = mm(x, tail_keys, "tn", P_MAP)
        maps_out[2 * b * D : 2 * (b + 1) * D, :] = both
        maps.append(both)
        decays.append(jnp.exp(end))
    for each in (inverse_out, x_out, maps_out):
        each.whole()

    def compose(first, first_decay, then, then_decay):
        moved = mm(first, then[0:D], passes=P_MAP)
        through = then_decay * first[0:D] + first_decay * then[0:D] - moved[0:D]
        added = then_decay * first[D:] - moved[D:] + then[D:]
        return jnp.concatenate([through, added], axis=0), first_decay * then_decay

    early, early_decay = compose(maps[0], decays[0], maps[1], decays[1])
    late, late_decay = compose(maps[2], decays[2], maps[3], decays[3])
    whole, decay = compose(early, early_decay, late, late_decay)
    whole = whole.astype(BF16)
    row = lax.broadcasted_iota(jnp.int32, (16, D), 0)
    decay = jnp.broadcast_to(decay, (16, D))
    high = decay.astype(BF16).astype(F32)
    low = (decay - high).astype(BF16).astype(F32)
    lowest = decay - high - low
    parts = jnp.where(row == 0, high, jnp.where(row == 1, low, jnp.where(row == 2, lowest, 0.0)))
    parts = parts.astype(BF16)
    for copy in range(packed.shape[0]):
        packed[copy, 0 : 2 * D, :] = whole
        packed[copy, 2 * D : PACK, :] = parts


def readout_kernel(scores, x, q, gates, read_out, base_out):
    columns = gate_columns(gates[...])
    for b in range(NB):
        px = mm(scores[block(b), :], x[block(b), :], passes=P_TY)
        grown = jnp.exp(columns[:, b : b + 1]) * q[block(b), :]
        read_out[2 * b * D : (2 * b + 1) * D, :] = grown - px[:, 0:D]
        read_out[(2 * b + 1) * D : 2 * (b + 1) * D, :] = -x[block(b), 0:D]
        base_out[2 * b * D : (2 * b + 1) * D, :] = px[:, D:]
        base_out[(2 * b + 1) * D : 2 * (b + 1) * D, :] = x[block(b), D:]


def back_kernel(ids, grad_own, grad_other, weight, back_out, mark):
    core = ids[1]
    mark.clear()
    weight.ready()
    head = weight[pl.ds(pl.multiple_of(core * D, D), D), :]
    back_out[pl.ds(pl.multiple_of(core * ROWS, ROWS), ROWS), :] = mm(grad_own[...], head, "nt")
    back_out[pl.ds(pl.multiple_of((1 - core) * ROWS, ROWS), ROWS), :] = mm(
        grad_other[...], head, "nt"
    )


def slab_decay(piece):
    return jnp.sum(piece[2 * D : PACK].astype(F32), axis=0, keepdims=True)


def forward_fold(gathered, first, last, state):
    def step(position, state):
        piece = gathered[position]
        return slab_decay(piece) * state + (
            piece[D : 2 * D].astype(F32) - mm(state, piece[0:D], passes=P_MAP)
        )

    return lax.fori_loop(first, last, step, state)


def backward_fold(gathered, gathered_grad, first, last, total):
    def step(count, total):
        position = last - 1 - count
        piece = gathered[position]
        return slab_decay(piece) * total + (
            gathered_grad[position, 0:D].astype(F32) - mm(total, piece[0:D], "nt", P_MAP)
        )

    return lax.fori_loop(0, last - first, step, total)


def forward_total_kernel(gathered, out):
    gathered.ready()
    out[...] = forward_fold(gathered, 0, gathered.shape[0], jnp.zeros((D, D), F32))


def backward_total_kernel(ids, gathered, gathered_grad, out, weight_here, weight_there):
    count = gathered.shape[0]
    out[...] = backward_fold(gathered, gathered_grad, 0, count, jnp.zeros((D, D), F32))
    height = weight_here.shape[0]
    total = gathered_grad[0, D:].astype(F32)
    for chip in range(1, count):
        total = total + gathered_grad[chip, D:].astype(F32)
    for part in range(weight_here.shape[1] // D):
        at = 2 * height * part
        first, second = total[at : at + height], total[at + height : at + 2 * height]
        weight_here[:, block(part)] = jnp.where(ids[2] == 0, first, second)
        weight_there[:, block(part)] = jnp.where(ids[2] == 0, second, first)


def outputs_kernel(
    ids, gathered, entry, maps, read, base, gates, back, gain, grad_own, grad_other,
    states_out, deltas_out, grads_out, reach_out, packed_grad, normed_out, sent, gain_out,
):
    chip, core = ids[0], ids[1]
    gathered.ready()
    state = forward_fold(gathered, 0, chip, entry[...])
    states, decays = [], []
    for b in range(NB):
        states.append(state)
        states_out[block(b), :] = state
        decay = jnp.exp(gates[b : b + 1, D - 1 : D])
        decays.append(decay)
        if b + 1 < NB:
            here = maps[2 * b * D : 2 * (b + 1) * D, :]
            state = decay * state - mm(state, here[0:D], passes=P_MAP) + here[D:]
    total_gain = jnp.zeros((1, D), F32)
    reaches = []
    for b in range(NB):
        both = slice(2 * b * D, 2 * (b + 1) * D)
        rows = base[both, :] + mm(read[both, :], states[b], "nt", P_OUT)
        out = rows[0:D]
        deltas_out[block(b), :] = rows[D:]
        inverse = lax.rsqrt(row_sum(out * out) * (1.0 / D) + EPS)
        unit_out = out * inverse
        normed = (unit_out * gain[0:1, :]).astype(BF16)
        normed_out[block(b), :] = normed

        @pl.when((b // 2) != core)
        def _():
            sent[block(b % 2), :] = normed

        cotangent = back[block(b), :]
        total_gain = total_gain + jnp.sum(cotangent * unit_out, axis=0, keepdims=True)
        scaled = cotangent * gain[0:1, :]
        grad = inverse * (scaled - unit_out * (row_sum(scaled * unit_out) * (1.0 / D)))
        grads_out[block(b), :] = grad
        reach = mm(grad, read[2 * b * D : (2 * b + 1) * D, :], "tn", P_OUT)
        reach_out[block(b), :] = reach
        reaches.append(reach)
    for each in (states_out, deltas_out, grads_out, reach_out, normed_out, sent):
        each.whole()
    gain_out[...] = jnp.broadcast_to(total_gain, (8, D))
    state_grad = reaches[NB - 1]
    for b in range(NB - 2, -1, -1):
        through = maps[2 * b * D : (2 * b + 1) * D, :]
        state_grad = decays[b] * state_grad - mm(state_grad, through, "nt", P_MAP) + reaches[b]
    state_grad = state_grad.astype(BF16)
    own, others = (pl.ds(pl.multiple_of(c * ROWS, ROWS), ROWS) for c in (core, 1 - core))
    share = mm(normed_out[own, :], grad_own[...], "tn")
    share = (share + mm(normed_out[others, :], grad_other[...], "tn")).astype(BF16)
    count = packed_grad.shape[0]
    height = D // (2 * count)
    for chip in range(count):
        packed_grad[chip, 0:D, :] = state_grad
        both = [share[height * c : height * (c + 1)] for c in (chip, count + chip)]
        rows = jnp.concatenate(both, axis=0)
        for part in range(share.shape[1] // D):
            at = D + 2 * height * part
            packed_grad[chip, at : at + 2 * height, :] = rows[:, block(part)]


def local_grads_kernel(
    scores, deltas, grads, states, q, k, gates,
    dq_out, dk_out, pull_out, rows_out, sums_out,
):
    columns = gate_columns(gates[...])
    i, j = grid_index()
    sums_out.clear()
    for b in range(NB):
        at = block(b)
        grad, score = grads[at, :], scores[at, :]
        damp = damping(columns[:, b : b + 1], gates[b : b + 1, :])
        d_score = jnp.where(i >= j, mm(grad, deltas[at, :], "nt", P_BACK), 0.0)
        d_inner = d_score * damp
        sums_out[b : b + 1, :] = jnp.sum(d_score * score, axis=0, keepdims=True)
        reading = mm(grad, states[at, :], passes=P_BACK)
        growth = jnp.exp(columns[:, b : b + 1])
        dq_out[at, :] = growth * reading + mm(d_inner, k[at, :], passes=P_BACK)
        dk_out[at, :] = mm(d_inner, q[at, :], "tn", P_BACK)
        pull_out[at, :] = mm(score, grad, "tn", P_BACK)
        row = row_sum(d_score * score) + row_sum(growth * q[at, :] * reading)
        rows_out[at, :] = jnp.broadcast_to(row, (D, D))


def grads_kernel(
    ids, gathered, gathered_grad, leaving, maps, reach, states, deltas, inverse, x, q, k, gates, pre, padded,
    dq, dk, pull, rows_in, sums, conv_w,
    keep_out, send_out, small_out, gate_keep,
    d_pre,
):
    chip, core = ids[0], ids[1]
    gathered.ready()
    gathered_grad.ready()
    exit_grad = backward_fold(
        gathered, gathered_grad, chip + 1, gathered.shape[0], leaving[...]
    )
    columns = gate_columns(gates[...])
    i, j = grid_index()
    strict = i > j
    exits = [None] * NB
    decays = [jnp.exp(gates[b : b + 1, D - 1 : D]) for b in range(NB)]
    for b in range(NB - 1, -1, -1):
        exits[b] = exit_grad
        if b:
            through = maps[2 * b * D : (2 * b + 1) * D, :]
            exit_grad = (
                decays[b] * exit_grad - mm(exit_grad, through, "nt", P_MAP) + reach[block(b), :]
            )
    d_pre[NB * D : NB * D + 8, :] = jnp.zeros((8, 3 * D), F32)
    lane = lax.broadcasted_iota(jnp.int32, (D, D), 1)
    row_terms = jnp.zeros((D, D), F32)
    beta_terms = jnp.zeros((D, D), F32)
    col_rows, end_rows = [], []
    for b in range(NB):
        at = block(b)
        key, query = k[at, :], q[at, :]
        cum, beta = columns[:, b : b + 1], columns[:, 4 + b : 5 + b]
        growth = jnp.exp(cum)
        remain = jnp.exp(gates[b : b + 1, D - 1 : D] - cum)
        damp = damping(cum, gates[b : b + 1, :])
        tail_keys = remain * key
        d_delta = pull[at, :] + mm(tail_keys, exits[b], "nt", P_BACK)
        d_x = jnp.concatenate([-mm(d_delta, states[at, :], passes=P_BACK), d_delta], axis=1)
        d_y = mm(inverse[at, :], d_x, "tn", P_BACK)
        both = x[at, :]
        d_lower = jnp.where(strict, -mm(d_y, both, "nt", P_BACK), 0.0)
        d_inner = d_lower * (beta * damp)
        inner = mm(key, key, "nt", P_KK)
        elementwise = d_inner * inner
        d_tail = mm(deltas[at, :], exits[b], passes=P_BACK)
        symmetric = d_inner + jnp.transpose(d_inner)
        d_key = (
            dk[at, :]
            + mm(symmetric, key, passes=P_BACK)
            + (beta * growth) * d_y[:, 0:D]
            + remain * d_tail
        )
        d_query = dq[at, :]
        tail_dot = row_sum(d_tail * tail_keys)
        written = row_sum((beta * growth) * key * d_y[:, 0:D])
        row = rows_in[at, :] + (row_sum(elementwise) + written - tail_dot)
        row_terms = jnp.where(lane == b, row, row_terms)
        beta_terms = jnp.where(lane == b, (1.0 - beta) * row_sum(d_y * both), beta_terms)
        col_rows.append(sums[b : b + 1, :] + jnp.sum(elementwise, axis=0, keepdims=True))
        end = jnp.sum(tail_dot, axis=0, keepdims=True) + decays[b] * jnp.sum(
            row_sum(exits[b] * states[at, :]), axis=0, keepdims=True
        )
        end_rows.append(jnp.broadcast_to(end, (1, D)))

        u_q, u_k, u_v = pre[at, 0:D], pre[at, D : 2 * D], pre[at, 2 * D :]
        sigmoids = [1.0 / (1.0 + jnp.exp(-u)) for u in (u_q, u_k, u_v)]
        raw_q = (u_q * sigmoids[0]).astype(BF16).astype(F32)
        raw_k = (u_k * sigmoids[1]).astype(BF16).astype(F32)
        unit_q, inverse_q = unit(raw_q)
        inverse_k = unit(raw_k)[1]
        d_unit = d_query * SCALE
        d_raw_q = inverse_q * (d_unit - unit_q * row_sum(unit_q * d_unit))
        d_raw_k = inverse_k * (d_key - key * row_sum(key * d_key))
        d_raw_v = beta * d_y[:, D:]
        for group, (d_raw, u, s) in enumerate(
            zip((d_raw_q, d_raw_k, d_raw_v), (u_q, u_k, u_v), sigmoids)
        ):
            d_pre[at, group * D : (group + 1) * D] = d_raw * (s * (1.0 + u * (1.0 - s)))

    rows = jnp.transpose(row_terms)[0:8, :] - jnp.concatenate(
        col_rows + [jnp.zeros((4, D), F32)], axis=0
    )
    d_decay = mm(rows, (i >= j).astype(F32), passes=6) + jnp.concatenate(
        end_rows + [jnp.zeros((4, D), F32)], axis=0
    )
    d_logit = jnp.transpose(beta_terms)[0:8, :]
    gate_keep.clear()
    small_out.clear()
    for target, top, own in ((gate_keep, 0, True), (small_out, 16, False)):
        for head in range(2):

            @pl.when(core == head)
            def _():
                first = 2 * (head if own else 1 - head)
                for half in range(2):
                    b = first + half
                    at = top + head
                    target[at : at + 1, block(half)] = d_decay[b : b + 1, :]
                    target[at + 2 : at + 3, block(half)] = d_logit[b : b + 1, :]

    keep_out.clear()
    send_out.clear()
    for group, lanes in enumerate(lane_groups(core)):
        here = slice(group * D, (group + 1) * D)
        taps = [conv_w[tap : tap + 1, lanes] for tap in range(4)]
        sums_of = [jnp.zeros((1, D), F32) for _ in range(4)]
        for b in range(NB):
            total = taps[3] * d_pre[b * D : (b + 1) * D, here]
            for tap in range(3):
                start = b * D + 3 - tap
                total = total + taps[tap] * d_pre[start : start + D, here]
            mine = (b // 2) == core
            at = slice((b % 2) * D, (b % 2 + 1) * D)

            @pl.when(mine)
            def _():
                keep_out[at, lanes] = total

            @pl.when(jnp.logical_not(mine))
            def _():
                send_out[at, lanes] = total.astype(BF16)

            for tap in range(4):
                start = 5 + tap + b * D
                sums_of[tap] = sums_of[tap] + jnp.sum(
                    d_pre[b * D : (b + 1) * D, here] * padded[start : start + D, here],
                    axis=0,
                    keepdims=True,
                )
        for tap in range(4):
            small_out[tap : tap + 1, lanes] = sums_of[tap]
        for back in range(1, 4):
            total = jnp.zeros((1, D), F32)
            for tap in range(0, 4 - back):
                at = 3 - back - tap
                total = total + taps[tap] * d_pre[at : at + 1, here]
            small_out[11 - back : 12 - back, lanes] = total


def shares_kernel(ids, normed, received, weight, gain_part, out, mark):
    core = ids[1]
    mark.clear()
    normed.ready()
    weight.ready()
    kept = normed[pl.ds(pl.multiple_of(core * ROWS, ROWS), ROWS), :]
    mine = weight[pl.ds(pl.multiple_of(core * D, D), D), :]
    others = weight[pl.ds(pl.multiple_of((1 - core) * D, D), D), :]
    share = (mm(kept, mine) + mm(received[...], others)).astype(BF16)
    count, height = out.shape[0], out.shape[1] - 16
    row = lax.broadcasted_iota(jnp.int32, (16, D), 0)
    gain = jnp.broadcast_to(gain_part[0:1, :], (16, D))
    high = gain.astype(BF16).astype(F32)
    extra = jnp.where(row == 0, high, jnp.where(row == 1, gain - high, 0.0)).astype(BF16)
    for owner in range(count):
        out[owner, 0:height, :] = share[owner * height : (owner + 1) * height]
        out[owner, height:, :] = jnp.zeros((16, out.shape[2]), BF16)
        out[owner, height:, 0:D] = extra


def call(kernel, shapes, args, name, flops, scratch=(), with_ids=True, after=(), near=(), limit=None):
    arrays = args[1:] if with_ids else args
    inputs = [any(x is other for other in near) for x in arrays]
    outputs = [len(each) > 2 for each in shapes]
    outs = [jax.ShapeDtypeStruct(each[0], each[1]) for each in shapes]
    anywhere, inside = (pl.BlockSpec(memory_space=space) for space in (pl.ANY, pltpu.VMEM))
    moved = sum(x.size * x.dtype.itemsize for x in [*arrays, *outs])
    buffers = [x for x, resident in zip([*arrays, *outs], inputs + outputs) if not resident]
    return pl.pallas_call(
        staged(kernel, inputs, len(after), outputs, with_ids),
        out_shape=outs,
        in_specs=[pl.BlockSpec(memory_space=pltpu.SMEM)] * with_ids
        + [inside if resident else anywhere for resident in inputs]
        + [anywhere] * len(after),
        out_specs=[inside if resident else anywhere for resident in outputs],
        scratch_shapes=[
            *[pltpu.VMEM(x.shape, x.dtype) for x in buffers],
            pltpu.SemaphoreType.DMA((max(1, inputs.count(False)),)),
            pltpu.SemaphoreType.DMA((max(1, outputs.count(False)),)),
            *scratch,
        ],
        name=name,
        cost_estimate=pl.CostEstimate(flops=flops, bytes_accessed=moved, transcendentals=0),
        compiler_params=pltpu.CompilerParams(vmem_limit_bytes=limit),
    )(*args, *after)


def everyone(x, axes):
    return lax.all_to_all(x, axes, 0, 0, tiled=True)


def local(mixed, log_decay, beta_logit, conv_weight, norm_gain, out_weight, out_grad):
    near, groups = lax.axis_size("near"), lax.axis_size("dp")
    chips = lax.axis_size("far") * near
    ids = jnp.stack([lax.axis_index(axis) for axis in ("near", "core", "far")]).astype(jnp.int32)
    chip_line, line = ("far", "near"), ("far", "near", "core")
    swap = [(0, 1), (1, 0)]
    width = out_weight.shape[1]
    rows = NB * D
    height = ROWS // groups

    gates_own = jnp.concatenate([log_decay.T, beta_logit.T, jnp.zeros((4, ROWS), F32)], axis=0)
    tail = mixed[ROWS - 16 :]
    tail_a = lax.ppermute(tail, line, [(2 * c + 1, 2 * c + 2) for c in range(chips - 1)])
    tail_b = lax.ppermute(tail, line, [(2 * c + 1, 2 * c + 3) for c in range(chips - 1)])
    other = lax.ppermute(mixed, "core", swap)
    gates_other = lax.ppermute(gates_own, "core", swap)
    grad_own = everyone(jnp.broadcast_to(out_grad[None], (groups, height, width)), "dp")
    grad_own = grad_own.reshape(ROWS, width)
    (padded, pre, q, k, inverse, x, scores, maps, gates, packed) = call(
        maps_kernel,
        [
            ((rows + 8, 3 * D), F32),
            ((rows, 3 * D), F32),
            ((rows, D), F32),
            ((rows, D), F32),
            ((rows, D), F32),
            ((rows, 2 * D), F32),
            ((rows, D), F32),
            ((2 * rows, D), F32),
            ((8, D), F32),
            ((near, PACK, D), BF16),
        ],
        [ids, mixed, other, tail_a, tail_b, gates_own, gates_other, conv_weight],
        "maps", 10**9, near=[other, tail_a, tail_b, gates_own, gates_other],
    )
    gathered = everyone(packed, "near")

    grad_other = lax.ppermute(grad_own, "core", swap)
    read, base = call(
        readout_kernel,
        [((2 * rows, D), F32), ((2 * rows, D), F32)],
        [scores, x, q, gates],
        "readout", 10**8, with_ids=False,
    )
    back, mark = call(
        back_kernel,
        [((rows, D), F32), ((8, D), F32)],
        [ids, grad_own, grad_other, out_weight],
        "back", 10**8, after=[read],
    )
    (total,) = call(
        forward_total_kernel,
        [((D, D), F32, "near")],
        [gathered],
        "forward_total", 10**8, with_ids=False, after=[mark], near=[gathered], limit=2**23,
    )
    entry = lax.ppermute(total, "far", [(0, 1)])
    gain = jnp.broadcast_to(norm_gain.reshape(1, D), (8, D))
    (states, deltas, grads, reach, packed_grad, normed, sent, gain_part) = call(
        outputs_kernel,
        [
            ((rows, D), F32),
            ((rows, D), F32),
            ((rows, D), F32),
            ((rows, D), F32),
            ((near, D + D // near * (width // D), D), BF16),
            ((rows, D), BF16),
            ((ROWS, D), BF16),
            ((8, D), F32),
        ],
        [ids, gathered, entry, maps, read, base, gates, back, gain, grad_own, grad_other],
        "outputs", 10**9, near=[gathered, entry, gain],
    )
    gathered_grad = everyone(packed_grad, "near")
    received = lax.ppermute(sent, "core", swap)
    dq, dk, pull, row_terms, sums = call(
        local_grads_kernel,
        [
            ((rows, D), F32),
            ((rows, D), F32),
            ((rows, D), F32),
            ((rows, D), F32),
            ((8, D), F32),
        ],
        [scores, deltas, grads, states, q, k, gates],
        "local_grads", 10**9, with_ids=False,
    )
    share, mark = call(
        shares_kernel,
        [((groups, height + 16, width), BF16), ((8, D), F32)],
        [ids, normed, received, out_weight, gain_part],
        "shares", 10**8, after=[sums], near=[received],
    )

    height_w = D // chips
    total, weight_here, weight_there = call(
        backward_total_kernel,
        [
            ((D, D), F32, "near"),
            ((height_w, width), F32, "near"),
            ((height_w, width), F32, "near"),
        ],
        [ids, gathered, gathered_grad],
        "backward_total", 10**8, near=[gathered, gathered_grad], after=[mark], limit=2**23,
    )
    leaving = lax.ppermute(total, "far", [(1, 0)])
    def owners(of_run):
        return [
            (2 * (f * near + n) + h, h * chips + of_run(f) * near + n)
            for f in range(2)
            for n in range(near)
            for h in range(2)
        ]

    weight_here = lax.ppermute(weight_here, line, owners(lambda f: f))
    weight_there = lax.ppermute(weight_there, line, owners(lambda f: 1 - f))
    leaving, share, weight_here, weight_there = lax.optimization_barrier(
        (leaving, share, weight_here, weight_there)
    )
    grad_weight = weight_here + weight_there

    keep, send, small, gate_keep = call(
        grads_kernel,
        [
            ((ROWS, 4 * D), F32),
            ((ROWS, 4 * D), BF16),
            ((24, 4 * D), F32, "near"),
            ((8, ROWS), F32, "near"),
        ],
        [
            ids, gathered, gathered_grad, leaving, maps, reach, states, deltas, inverse, x, q, k, gates,
            pre, padded, dq, dk, pull, row_terms, sums, conv_weight,
        ],
        "grads", 10**9, near=[gathered, gathered_grad, leaving],
        scratch=[pltpu.VMEM((rows + 8, 3 * D), F32)],
    )
    shares = everyone(share, "dp").astype(F32)
    result = jnp.sum(shares[:, :height], axis=0).astype(BF16)
    gain_rows = jnp.sum(shares[:, height : height + 2, :D], axis=0)

    gain_row = gain_rows[0:1] + gain_rows[1:2]
    small = small + jnp.pad(gain_row, ((4, 19), (0, 3 * D)))
    small_other = lax.ppermute(small, "core", swap)
    gate_taken = small_other[16:24, :ROWS]
    spill = small[8:16] + small_other[8:16]
    totals = small[0:8] + small_other[0:8]
    totals, spill, send = lax.optimization_barrier((totals, spill, send))
    taken = lax.ppermute(send, "core", swap)
    spilled = lax.ppermute(spill, line, [(2 * c + 1, 2 * c - 1) for c in range(1, chips)])
    distance = 1
    while distance < chips:
        pairs = [(c, c ^ distance) for c in range(chips)]
        seen = lax.ppermute(totals, chip_line, pairs)
        last = distance * 2 == chips
        if not last:
            totals = totals + seen
        distance *= 2
    grad_taps = totals[0:4] + seen[0:4]
    grad_gain = totals[4, :D] + seen[4, :D]

    spilled = jnp.pad(spilled[0:3], ((ROWS - 3, 0), (0, 0)))
    grad_mixed = (keep + taken.astype(F32) + spilled).astype(BF16)
    gate_grads = gate_keep + gate_taken
    return (
        result,
        grad_mixed,
        gate_grads[0:2].T,
        gate_grads[2:4].T,
        grad_taps,
        grad_gain,
        grad_weight,
    )


def solution(mesh):
    groups, line = mesh.shape["dp"], mesh.shape["ctx"]
    ctx = ("far", "near", "core")
    fine = Mesh(mesh.devices.reshape(groups, 2, line // 4, 2), ("dp", *ctx))
    return jax.shard_map(
        local,
        mesh=fine,
        in_specs=(
            P(ctx, "dp"),
            P(ctx, "dp"),
            P(ctx, "dp"),
            P(None, "dp"),
            P(),
            P("dp", None),
            P((*ctx, "dp"), None),
        ),
        out_specs=(
            P((*ctx, "dp"), None),
            P(ctx, "dp"),
            P(ctx, "dp"),
            P(ctx, "dp"),
            P(None, "dp"),
            P(),
            P(("dp", *ctx), None),
        ),
        check_vma=False,
    )
```
